32 devices in a mesh: row: 4 (over z), col: 8 (over y, x, core).
Axes of the slice: x: 2, y: 2, z: 4, core: 2. Of those that a mesh axis runs over, the one named last changes fastest.
Arguments:
- tokens: bfloat16 [2, 96, 128, 512], P(None, 'row', 'col'), may hold values from -6 to 6
- w_qkv: bfloat16 [512, 1536], replicated, may hold values from -0.25 to 0.25
- w_out: bfloat16 [512, 512], replicated, may hold values from -0.25 to 0.25
- q_saved: bfloat16 [2, 96, 128, 512], P(None, 'row', 'col'), may hold values from -4 to 4
- k_saved: bfloat16 [2, 96, 128, 512], P(None, 'row', 'col'), may hold values from -4 to 4
- v_saved: bfloat16 [2, 96, 128, 512], P(None, 'row', 'col'), may hold values from -4 to 4
- scale_exp: int32 [2, 12, 16, 24], P(None, 'row', 'col'), may hold values from -1 to 1
- grad_out: bfloat16 [2, 96, 128, 512], P(None, 'row', 'col'), may hold values from -6 to 6
- crop_start: int32 [2, 2], replicated, may hold values from 0 to 3
Outputs:
- grad_tokens: bfloat16 [2, 96, 128, 512], P(None, 'row', 'col')
- grad_w_qkv: float32 [512, 1536], P('row', 'col')
- grad_w_out: float32 [512, 512], P('row', 'col')
The draws below stay inside these ranges and needn't reach their ends.
Inputs may be any that keep to these rules, and one draw needn't show every extreme that they name: crop_start[b] holds the first row and the first column of the region of frame b that the loss covers.
All inputs are finite; a program needn't handle non-finite values.
Results may differ from the reference program's by a relative error of at most 0.017.
Values may be sent and summed in bfloat16 or wider, within the bound.
A program may use at most 128 MiB of HBM per device.

```python
import math
import jax
import jax.numpy as jnp
from jax import lax

WIDTH = 512
HEADS = 8
RADIUS = 4
BLOCK = 8
BATCH = 2
FRAME_ROWS = 96
FRAME_COLS = 128


def draw_q_saved(key, part):
    shape = (BATCH, FRAME_ROWS, FRAME_COLS, WIDTH)
    own_key = jax.random.fold_in(key, 11)
    return jnp.clip(jax.random.normal(own_key, shape, jnp.float32), -4.0, 4.0).astype(jnp.bfloat16)


def draw_k_saved(key, part):
    shape = (BATCH, FRAME_ROWS, FRAME_COLS, WIDTH)
    own_key = jax.random.fold_in(key, 13)
    return jnp.clip(jax.random.normal(own_key, shape, jnp.float32), -4.0, 4.0).astype(jnp.bfloat16)


def touch_ends(array, key, least, top_value):
    shape = array.shape
    place = [jax.random.randint(jax.random.fold_in(key, axis), (), 0, shape[axis]) for axis in range(len(shape))]
    array = array.at[tuple(place)].set(least)
    longest = shape.index(max(shape))
    place[longest] = (place[longest] + 1) % shape[longest]
    return array.at[tuple(place)].set(top_value)


def strengthened(result, key, source, target, shards_of, factor):
    def block_of(dim):
        return (jnp.arange(result.shape[dim]) // (result.shape[dim] // shards_of)).reshape((-1,) + (1,) * (result.ndim - 1 - dim))

    one_side = jax.random.permutation(key, shards_of)[block_of(target)]
    other_side = (block_of(target) + shards_of // 2) % shards_of
    return jnp.where((block_of(source) == one_side) | (block_of(source) == other_side), factor * result, result)


def block_scale(rng, dims, shards, least, largest):
    level, own = 1.0, jax.random.fold_in(rng, 6)
    for axis_at, shards_of in shards:
        heights = jnp.exp(jax.random.uniform(jax.random.fold_in(own, axis_at), (shards_of,), jnp.float32, least / len(shards), largest / len(shards)))
        level = level * jnp.repeat(heights, dims[axis_at] // shards_of).reshape([-1 if axis == axis_at else 1 for axis in range(len(dims))])
    return level


def scatter_about(rng, shape, deviation, most, cuts=(), held_as=jnp.bfloat16):
    result = deviation * jax.random.normal(rng, shape, jnp.float32)
    if cuts:
        result = result * block_scale(rng, shape, cuts, -0.22, 0.18)
    return jnp.clip(result, -most, most).astype(held_as)


def gaussian_with(stream_key, dims, spread, most, shards, heavy, kind=jnp.bfloat16):
    drawn = spread * jax.random.normal(stream_key, dims, jnp.float32)
    if shards:
        drawn = drawn * block_scale(stream_key, dims, shards, -0.22, 0.18)
    return jnp.clip(strengthened(drawn, jax.random.fold_in(stream_key, 3), *heavy), -most, most).astype(kind)


def setup_inputs(seed: int = 0) -> dict:
    key_of = jax.random.split(jax.random.key(seed), 10)
    tokens = gaussian_with(key_of[0], (BATCH, FRAME_ROWS, FRAME_COLS, WIDTH), 1.0, 6.0, ((1, 4), (2, 8)), (1, 3, 4, 2.0))
    w_qkv = scatter_about(key_of[1], (WIDTH, 3 * WIDTH), WIDTH ** -0.5, 0.25)
    w_out = scatter_about(key_of[2], (WIDTH, WIDTH), WIDTH ** -0.5, 0.25)
    q_saved = draw_q_saved(jax.random.fold_in(key_of[9], 71), 0)
    k_saved = draw_k_saved(jax.random.fold_in(key_of[9], 71), 0)
    v_saved = scatter_about(key_of[5], (BATCH, FRAME_ROWS, FRAME_COLS, WIDTH), 1.0, 4.0, ((1, 4), (2, 8)))
    scale_exp = touch_ends(jax.random.randint(key_of[6], (BATCH, FRAME_ROWS // BLOCK, FRAME_COLS // BLOCK, 3 * HEADS), -1, 2), jax.random.fold_in(key_of[6], 1), -1, 1).astype(jnp.int32)
    grad_out = gaussian_with(key_of[7], (BATCH, FRAME_ROWS, FRAME_COLS, WIDTH), 1.0, 6.0, ((1, 4), (2, 8)), (2, 3, 8, 2.0))
    crop_start = touch_ends(jax.random.randint(key_of[8], (BATCH, 2), 0, RADIUS), jax.random.fold_in(key_of[8], 1), 0, RADIUS - 1).astype(jnp.int32)
    return dict(tokens=tokens, w_qkv=w_qkv, w_out=w_out, q_saved=q_saved, k_saved=k_saved, v_saved=v_saved, scale_exp=scale_exp, grad_out=grad_out, crop_start=crop_start)


max_norm = 1000.0
masked_score = -1e+30
tiny_square = 1e-06

def product(form, left, right):
    return jnp.einsum(form, left.astype(jnp.float32), right.astype(jnp.float32))

def dequantize(mantissa, exponent):
    members, height, breadth, features = mantissa.shape
    heads = exponent.shape[3]
    factor = jnp.exp2(exponent.astype(jnp.float32))
    factor = jnp.repeat(jnp.repeat(factor, BLOCK, axis=1), BLOCK, axis=2)
    scaled = mantissa.astype(jnp.float32).reshape(members, height, breadth, heads, features // heads) * factor[..., None]
    return scaled.reshape(members, height, breadth, features).astype(jnp.bfloat16)

def query_tiles(tensor):
    height, breadth, features = tensor.shape
    blocked = tensor.reshape(height // BLOCK, BLOCK, breadth // BLOCK, BLOCK, HEADS, features // HEADS)
    return blocked.transpose(0, 2, 1, 3, 4, 5).reshape(height // BLOCK, breadth // BLOCK, BLOCK * BLOCK, HEADS, features // HEADS)

def query_untile(tile_set, height, breadth):
    tile_rows, tile_cols = (tile_set.shape[0], tile_set.shape[1])
    features = tile_set.shape[3] * tile_set.shape[4]
    blocked = tile_set.reshape(tile_rows, tile_cols, BLOCK, BLOCK, features)
    return blocked.transpose(0, 2, 1, 3, 4).reshape(height, breadth, features)

def key_tiles(padded):
    height, breadth, features = padded.shape
    tile_rows = height // BLOCK - 1
    tile_cols = breadth // BLOCK - 1
    blocked = padded.reshape(tile_rows + 1, BLOCK, tile_cols + 1, BLOCK, features)
    paired = jnp.stack([blocked[:-1], blocked[1:]], axis=1).reshape(tile_rows, 2 * BLOCK, tile_cols + 1, BLOCK, features)
    paired = jnp.stack([paired[:, :, :-1], paired[:, :, 1:]], axis=3).reshape(tile_rows, 2 * BLOCK, tile_cols, 2 * BLOCK, features)
    return paired.transpose(0, 2, 1, 3, 4).reshape(tile_rows, tile_cols, 4 * BLOCK * BLOCK, HEADS, features // HEADS)

def fold_keys(tile_set):
    tile_rows, tile_cols = (tile_set.shape[0], tile_set.shape[1])
    features = tile_set.shape[3] * tile_set.shape[4]
    tile_grid = tile_set.reshape(tile_rows, tile_cols, 2, BLOCK, 2, BLOCK, features).transpose(0, 2, 3, 1, 4, 5, 6)
    zero_row = jnp.zeros((1, BLOCK, tile_cols, 2, BLOCK, features), tile_set.dtype)
    summed = jnp.concatenate([tile_grid[:, 0], zero_row], 0) + jnp.concatenate([zero_row, tile_grid[:, 1]], 0)
    zero_col = jnp.zeros((tile_rows + 1, BLOCK, 1, BLOCK, features), tile_set.dtype)
    summed = jnp.concatenate([summed[:, :, :, 0], zero_col], 2) + jnp.concatenate([zero_col, summed[:, :, :, 1]], 2)
    return summed.reshape((tile_rows + 1) * BLOCK, (tile_cols + 1) * BLOCK, features)

def key_valid(anchor, tile_count, extent):
    position = anchor + BLOCK * jnp.arange(tile_count, dtype=jnp.int32)[:, None] + jnp.arange(2 * BLOCK, dtype=jnp.int32)[None, :]
    return (position >= 0) & (position < extent)

def window_mask():
    reach = jnp.arange(2 * BLOCK, dtype=jnp.int32)[None, :] - jnp.arange(BLOCK, dtype=jnp.int32)[:, None]
    inside = (reach >= 0) & (reach <= 2 * RADIUS)
    return (inside[:, None, :, None] & inside[None, :, None, :]).reshape(BLOCK * BLOCK, 4 * BLOCK * BLOCK)

def attend(queries, grads_attn, keys_pad, values_pad, row_anchor, col_anchor, frame_rows, frame_cols):
    height, breadth, features = queries.shape
    score_scale = 1.0 / math.sqrt(features // HEADS)
    q_tiles = query_tiles(queries)
    g_tiles = query_tiles(grads_attn)
    k_tiles = key_tiles(keys_pad)
    v_tiles = key_tiles(values_pad)
    tile_rows, tile_cols = (q_tiles.shape[0], q_tiles.shape[1])
    row_ok = key_valid(row_anchor, tile_rows, frame_rows)
    col_ok = key_valid(col_anchor, tile_cols, frame_cols)
    keys_ok = (row_ok[:, None, :, None] & col_ok[None, :, None, :]).reshape(tile_rows, tile_cols, 1, 1, 4 * BLOCK * BLOCK)
    allowed = keys_ok & window_mask()[None, None, None]
    scores = product('ijqhd,ijkhd->ijhqk', q_tiles, k_tiles) * score_scale
    scores = jnp.where(allowed, scores, masked_score)
    row_max = lax.optimization_barrier(jnp.max(scores, axis=-1, keepdims=True))
    weights = jnp.exp(scores - row_max)
    softmax = weights / lax.optimization_barrier(jnp.sum(weights, axis=-1, keepdims=True))
    softmax_half = softmax.astype(jnp.bfloat16)
    out_tiles = product('ijhqk,ijkhd->ijqhd', softmax_half, v_tiles).astype(jnp.bfloat16)
    row_delta = product('ijqhd,ijqhd->ijhq', g_tiles, out_tiles)
    grad_probs = product('ijqhd,ijkhd->ijhqk', g_tiles, v_tiles)
    grad_scores = (softmax * (grad_probs - row_delta[..., None]) * score_scale).astype(jnp.bfloat16)
    grad_q_tiles = product('ijhqk,ijkhd->ijqhd', grad_scores, k_tiles)
    grad_k_tiles = product('ijhqk,ijqhd->ijkhd', grad_scores, q_tiles)
    grad_v_tiles = product('ijhqk,ijqhd->ijkhd', softmax_half, g_tiles)
    return (query_untile(out_tiles, height, breadth), query_untile(grad_q_tiles, height, breadth), fold_keys(grad_k_tiles), fold_keys(grad_v_tiles))

def reference(tokens, w_qkv, w_out, q_saved, k_saved, v_saved, scale_exp, grad_out, crop_start):
    members, height, breadth, features = tokens.shape
    queries = dequantize(q_saved, scale_exp[..., :HEADS])
    keys_full = dequantize(k_saved, scale_exp[..., HEADS:2 * HEADS])
    values = dequantize(v_saved, scale_exp[..., 2 * HEADS:])
    row_place = jnp.arange(height, dtype=jnp.int32)
    col_place = jnp.arange(breadth, dtype=jnp.int32)
    inside = (row_place[None, :, None] >= crop_start[:, 0][:, None, None]) & (col_place[None, None, :] >= crop_start[:, 1][:, None, None])
    masked = jnp.where(inside[..., None], grad_out, jnp.zeros_like(grad_out))
    flat_grad = masked.reshape(-1, features)
    grad_attn = jnp.dot(flat_grad, w_out.T, preferred_element_type=jnp.float32).astype(jnp.bfloat16).reshape(masked.shape)
    padding = ((RADIUS, RADIUS), (RADIUS, RADIUS), (0, 0))

    def one_member(member):
        q_member, g_member, k_member, v_member = member
        keys_pad = jnp.pad(k_member, padding)
        values_pad = jnp.pad(v_member, padding)

        def strip_step(running, strip_index):
            row_start = (strip_index * BLOCK).astype(jnp.int32)
            anchor_zero = jnp.zeros((), jnp.int32)
            q_strip = lax.dynamic_slice_in_dim(q_member, row_start, BLOCK, 0)
            g_strip = lax.dynamic_slice_in_dim(g_member, row_start, BLOCK, 0)
            k_strip = lax.dynamic_slice_in_dim(keys_pad, row_start, 2 * BLOCK, 0)
            v_strip = lax.dynamic_slice_in_dim(values_pad, row_start, 2 * BLOCK, 0)
            out_strip, grad_q_strip, grad_k_strip, grad_v_strip = attend(q_strip, g_strip, k_strip, v_strip, row_start - RADIUS, -RADIUS, height, breadth)
            grad_k_sum, grad_v_sum = running
            corner = (row_start, anchor_zero, anchor_zero)
            grad_k_sum = lax.dynamic_update_slice(grad_k_sum, lax.dynamic_slice(grad_k_sum, corner, grad_k_strip.shape) + grad_k_strip, corner)
            grad_v_sum = lax.dynamic_update_slice(grad_v_sum, lax.dynamic_slice(grad_v_sum, corner, grad_v_strip.shape) + grad_v_strip, corner)
            return ((grad_k_sum, grad_v_sum), (out_strip, grad_q_strip))
        initial = (jnp.zeros(keys_pad.shape, jnp.float32), jnp.zeros(values_pad.shape, jnp.float32))
        (grad_k_sum, grad_v_sum), (out_strips, grad_q_strips) = lax.scan(strip_step, initial, jnp.arange(height // BLOCK, dtype=jnp.int32))
        return (out_strips.reshape(height, breadth, features), grad_q_strips.reshape(height, breadth, features), grad_k_sum[RADIUS:RADIUS + height, RADIUS:RADIUS + breadth], grad_v_sum[RADIUS:RADIUS + height, RADIUS:RADIUS + breadth])
    attn_out, grad_query, grad_key, grad_value = lax.map(one_member, (queries, grad_attn, keys_full, values))
    flat_qkv = jnp.concatenate([grad_query, grad_key, grad_value], axis=-1).astype(jnp.bfloat16).reshape(-1, 3 * features)
    grad_tokens = jnp.dot(flat_qkv, w_qkv.T, preferred_element_type=jnp.float32).astype(jnp.bfloat16).reshape(tokens.shape)
    raw_qkv = jnp.dot(tokens.reshape(-1, features).T, flat_qkv, preferred_element_type=jnp.float32)
    raw_out = jnp.dot(attn_out.reshape(-1, features).T, flat_grad, preferred_element_type=jnp.float32)
    squares = jnp.sum(raw_qkv * raw_qkv) + jnp.sum(raw_out * raw_out)
    factor = jnp.minimum(1.0, max_norm / jnp.sqrt(squares + tiny_square))
    return (grad_tokens, factor * raw_qkv, factor * raw_out)
```

```python
import functools
import math

import jax
import jax.numpy as jnp
from jax import lax
from jax.experimental import pallas as pl
from jax.experimental.pallas import tpu as pltpu
from jax.sharding import PartitionSpec as P

HEADS = 8
RADIUS = 4
BLOCK = 8

max_norm = 1000.0
masked_score = -1e30
tiny_square = 1e-06
F32 = jnp.float32
BF16 = jnp.bfloat16


def dot(left, right, dims):
    return lax.dot_general(left, right, (dims, ((), ())), preferred_element_type=F32)


def prepare_kernel(q_ref, k_ref, v_ref, g_ref, fac_ref, crop_ref, w_ref,
                   q_out, kv_out, g_out, do_out, *, breadth):
    frame = pl.program_id(0)
    strip = pl.program_id(1)
    cells, features = q_ref.shape[1:]
    height = BLOCK * pl.num_programs(1)
    cell = lax.broadcasted_iota(jnp.int32, (cells, features), 0)
    block_col = (cell % breadth) // BLOCK

    def factor_of(which):
        factor = fac_ref[0, 0, 0:1, which * features:(which + 1) * features]
        full = jnp.broadcast_to(factor, (cells, features))
        for at in range(1, breadth // BLOCK):
            factor = fac_ref[0, 0, at:at + 1, which * features:(which + 1) * features]
            full = jnp.where(block_col == at, factor, full)
        return full

    q_out[0] = (q_ref[0].astype(F32) * factor_of(0)).astype(BF16)
    kv_out[0, 0] = (k_ref[0].astype(F32) * factor_of(1)).astype(BF16)
    kv_out[1, 0] = (v_ref[0].astype(F32) * factor_of(2)).astype(BF16)
    row = lax.axis_index("row") * height + strip * BLOCK + cell // breadth
    col = lax.axis_index("col") * breadth + cell % breadth
    inside = (row >= crop_ref[frame, 0]) & (col >= crop_ref[frame, 1])
    masked = jnp.where(inside, g_ref[0].astype(F32), 0.0).astype(BF16)
    g_out[0] = masked
    do_out[0] = dot(masked, w_ref[...], ((1,), (1,))).astype(BF16)


def prepare(q, k, v, g, factors, crop_start, w_out, breadth):
    members, cells, features = q.shape
    strip_cells = BLOCK * breadth
    strips = cells // strip_cells
    spec = pl.BlockSpec((1, strip_cells, features), lambda b, t: (b, t, 0))
    kv_spec = pl.BlockSpec((2, 1, strip_cells, features), lambda b, t: (0, b, t, 0))
    shape = jax.ShapeDtypeStruct(q.shape, BF16)
    return pl.pallas_call(
        functools.partial(prepare_kernel, breadth=breadth),
        grid=(members, strips),
        in_specs=[spec, spec, spec, spec,
                  pl.BlockSpec((1, 1) + factors.shape[2:], lambda b, t: (b, t, 0, 0)),
                  pl.BlockSpec(memory_space=pltpu.SMEM),
                  pl.BlockSpec(w_out.shape, lambda b, t: (0, 0))],
        out_specs=[spec, kv_spec, spec, spec],
        out_shape=[shape, jax.ShapeDtypeStruct((2,) + q.shape, BF16), shape, shape],
        name="prepare",
    )(q, k, v, g, factors, crop_start, w_out)


def attend_kernel(q_ref, do_ref, kvc_ref, kvs_ref, ot_ref, dq_ref, dc_ref, ds_ref, bias_ref,
                  *, breadth, head_dim):
    strip_cells = BLOCK * breadth
    side_cells = BLOCK * 2 * RADIUS
    strips = q_ref.shape[1] // strip_cells
    keys_c, keys_s = 2 * strip_cells, 2 * side_cells
    keys = keys_c + keys_s
    lanes = q_ref.shape[2]
    stacked = (lanes // head_dim) * strip_cells
    height = strips * BLOCK

    @pl.when((pl.program_id(0) == 0) & (pl.program_id(1) == 0))
    def _():
        key = lax.broadcasted_iota(jnp.int32, (keys, stacked), 0)
        query = lax.broadcasted_iota(jnp.int32, (keys, stacked), 1) % strip_cells
        side = key - keys_c
        key_row = jnp.where(key < keys_c, key // breadth, side // (2 * RADIUS)) - RADIUS
        along = side % (2 * RADIUS)
        key_col = jnp.where(
            key < keys_c, key % breadth,
            jnp.where(along < RADIUS, along - RADIUS, along - RADIUS + breadth))
        d_row = key_row - query // breadth
        d_col = key_col - query % breadth
        near = (jnp.abs(d_row) <= RADIUS) & (jnp.abs(d_col) <= RADIUS)
        frame_rows = height * lax.axis_size("row")
        frame_cols = breadth * lax.axis_size("col")
        at_col = key_col + lax.axis_index("col") * breadth
        near = near & (at_col >= 0) & (at_col < frame_cols)
        for strip in range(strips):
            at_row = key_row + strip * BLOCK + lax.axis_index("row") * height
            seen = near & (at_row >= 0) & (at_row < frame_rows)
            bias_ref[strip] = jnp.where(seen, 0.0, masked_score)

    lane = lax.broadcasted_iota(jnp.int32, (strip_cells, lanes), 1)
    masks = [jnp.where(lane // head_dim == h, 1.0, 0.0).astype(BF16)
             for h in range(lanes // head_dim)]
    scale = 1.0 / math.sqrt(head_dim)

    def by_head(whole):
        return jnp.concatenate(
            [whole[h * head_dim:(h + 1) * head_dim, h * strip_cells:(h + 1) * strip_cells]
             for h in range(lanes // head_dim)], 0)

    carry = None
    for strip in range(strips):
        at = slice(strip * strip_cells, (strip + 1) * strip_cells)
        at_c = slice(strip * strip_cells, strip * strip_cells + keys_c)
        at_s = slice(strip * side_cells, strip * side_cells + keys_s)
        q = q_ref[0, at] * scale
        g = do_ref[0, at]
        q_stack = jnp.concatenate([q * m for m in masks], 0)
        g_stack = jnp.concatenate([g * m for m in masks], 0)
        k = jnp.concatenate([kvc_ref[0, 0, at_c], kvs_ref[0, 0, at_s]], 0)
        v = jnp.concatenate([kvc_ref[1, 0, at_c], kvs_ref[1, 0, at_s]], 0)
        scores = dot(k, q_stack, ((1,), (1,))) + bias_ref[strip]
        weights = jnp.exp(scores - jnp.max(scores, axis=0, keepdims=True))
        softmax = weights * (1.0 / jnp.sum(weights, axis=0, keepdims=True))
        half = softmax.astype(BF16)
        grad_probs = dot(v, g_stack, ((1,), (1,)))
        delta = jnp.sum(softmax * grad_probs, axis=0, keepdims=True)
        grad_scores = (softmax * (grad_probs - delta)).astype(BF16)
        ot_ref[:, at] = by_head(dot(v, half, ((0,), (0,)))).astype(BF16)
        dq = by_head(dot(k, grad_scores, ((0,), (0,)))) * scale
        dq_ref[0, at] = dq.T.astype(BF16)
        parts = (dot(grad_scores, q_stack, ((1,), (0,))), dot(half, g_stack, ((1,), (0,))))
        for which in range(2):
            part_c, part_s = parts[which][:keys_c], parts[which][keys_c:]
            first_c, first_s = part_c[:strip_cells], part_s[:side_cells]
            if carry is not None:
                first_c = first_c + carry[which][0]
                first_s = first_s + carry[which][1]
            dc_ref[which, 0, at] = first_c
            ds_ref[which, 0, strip * side_cells:(strip + 1) * side_cells] = first_s.astype(BF16)
        carry = [(p[strip_cells:keys_c], p[keys_c + side_cells:]) for p in parts]
    for which in range(2):
        dc_ref[which, 0, strips * strip_cells:] = carry[which][0]
        ds_ref[which, 0, strips * side_cells:] = carry[which][1].astype(BF16)


def attend(q, do, kv_c, kv_s, breadth):
    members, cells, features = q.shape
    head_dim = features // HEADS
    lanes = 128
    strips = cells // (BLOCK * breadth)
    keys = 2 * BLOCK * (breadth + 2 * RADIUS)
    stacked = (lanes // head_dim) * BLOCK * breadth
    spec = pl.BlockSpec((1, cells, lanes), lambda b, h: (b, 0, h))

    def kv_spec(array):
        return pl.BlockSpec((2, 1, array.shape[2], lanes), lambda b, h: (0, b, 0, h))

    return pl.pallas_call(
        functools.partial(attend_kernel, breadth=breadth, head_dim=head_dim),
        grid=(members, features // lanes),
        in_specs=[spec, spec, kv_spec(kv_c), kv_spec(kv_s)],
        out_specs=[pl.BlockSpec((lanes, cells), lambda b, h: (h, b)), spec,
                   kv_spec(kv_c), kv_spec(kv_s)],
        out_shape=[jax.ShapeDtypeStruct((features, members * cells), BF16),
                   jax.ShapeDtypeStruct(q.shape, BF16),
                   jax.ShapeDtypeStruct(kv_c.shape, F32),
                   jax.ShapeDtypeStruct(kv_s.shape, BF16)],
        scratch_shapes=[pltpu.VMEM((strips, keys, stacked), F32)],
        name="attend",
    )(q, do, kv_c, kv_s)


def passed_along(array, axis, by):
    size = lax.axis_size(axis)
    return lax.ppermute(
        array, axis, [(i, i + by) for i in range(size) if 0 <= i + by < size])


def body(tokens, w_qkv, w_out, q_saved, k_saved, v_saved, scale_exp, grad_out, crop_start):
    members, height, breadth, features = tokens.shape
    cells = height * breadth
    rows, cols = lax.axis_size("row"), lax.axis_size("col")
    factors = jnp.repeat(jnp.exp2(scale_exp.astype(F32)), features // HEADS, axis=3)

    def flat(array):
        return array.reshape(members, cells, features)

    q, kv, g, do = prepare(flat(q_saved), flat(k_saved), flat(v_saved), flat(grad_out),
                           factors, crop_start, w_out, breadth)
    edge = RADIUS * breadth
    kv_c = jnp.concatenate(
        [passed_along(kv[:, :, -edge:], "row", 1), kv,
         passed_along(kv[:, :, :edge], "row", -1)], axis=2)
    grid = kv_c.reshape(2, members, height + 2 * RADIUS, breadth, features)
    kv_s = jnp.concatenate(
        [passed_along(grid[:, :, :, -RADIUS:], "col", 1),
         passed_along(grid[:, :, :, :RADIUS], "col", -1)], axis=3)
    kv_s = kv_s.reshape(2, members, -1, features)
    o_t, dq, d_c, d_s = attend(q, do, kv_c, kv_s, breadth)
    d_c = d_c.reshape(2, members, height + 2 * RADIUS, breadth, features)
    d_s = d_s.reshape(2, members, height + 2 * RADIUS, 2 * RADIUS, features)
    from_left = passed_along(d_s[:, :, :, RADIUS:], "col", 1)
    from_right = passed_along(d_s[:, :, :, :RADIUS], "col", -1)
    gap = jnp.zeros(d_s.shape[:3] + (breadth - 2 * RADIUS, features), BF16)
    d_c = d_c + jnp.concatenate([from_left, gap, from_right], axis=3).astype(F32)
    from_up = passed_along(d_c[:, :, -RADIUS:].astype(BF16), "row", 1)
    from_down = passed_along(d_c[:, :, :RADIUS].astype(BF16), "row", -1)
    gap = jnp.zeros((2, members, height - 2 * RADIUS, breadth, features), BF16)
    owned = d_c[:, :, RADIUS:-RADIUS] + jnp.concatenate(
        [from_up, gap, from_down], axis=2).astype(F32)
    owned = owned.astype(BF16).reshape(2, members * cells, features)
    flat_qkv = jnp.concatenate([dq.reshape(-1, features), owned[0], owned[1]], axis=1)
    grad_tokens = dot(flat_qkv, w_qkv, ((1,), (1,))).astype(BF16).reshape(tokens.shape)
    raw_qkv = dot(tokens.reshape(-1, features), flat_qkv, ((0,), (0,))).astype(BF16)
    raw_out = dot(o_t, g.reshape(-1, features), ((1,), (0,))).astype(BF16)
    pieces = jnp.concatenate(
        [raw.reshape(rows, features // rows, cols, -1).transpose(0, 2, 1, 3)
         for raw in (raw_qkv, raw_out)], axis=3)
    pieces = pieces.reshape((rows * cols,) + pieces.shape[2:])
    part = lax.psum_scatter(pieces, ("row", "col"), scatter_dimension=0, tiled=False)
    part = part.astype(F32)
    squares = lax.psum(jnp.sum(part * part), ("row", "col"))
    factor = jnp.minimum(1.0, max_norm / jnp.sqrt(squares + tiny_square))
    part = factor * part
    split = 3 * features // cols
    return grad_tokens, part[:, :split], part[:, split:]


def solution(mesh):
    placed = (
        P(None, "row", "col", None), P(), P(),
        P(None, "row", "col", None), P(None, "row", "col", None),
        P(None, "row", "col", None), P(None, "row", "col", None),
        P(None, "row", "col", None), P(),
    )
    return jax.shard_map(
        body, mesh=mesh, in_specs=placed,
        out_specs=(P(None, "row", "col", None), P("row", "col"), P("row", "col")),
        check_vma=False)
```

```python
import functools
import math

import jax
import jax.numpy as jnp
from jax import lax
from jax.experimental import pallas as pl
from jax.experimental.pallas import tpu as pltpu
from jax.sharding import PartitionSpec as P

HEADS = 8
RADIUS = 4
BLOCK = 8

max_norm = 1000.0
masked_score = -1e30
tiny_square = 1e-06
F32 = jnp.float32
BF16 = jnp.bfloat16


def dot(left, right, dims):
    return lax.dot_general(left, right, (dims, ((), ())), preferred_element_type=F32)


def prepare_kernel(q_ref, k_ref, v_ref, g_ref, fac_ref, crop_ref, w_ref,
                   q_out, kv_out, g_out, do_out, *, breadth):
    frame = pl.program_id(0)
    strip = pl.program_id(1)
    cells, features = q_ref.shape[1:]
    height = BLOCK * pl.num_programs(1)
    cell = lax.broadcasted_iota(jnp.int32, (cells, features), 0)
    block_col = (cell % breadth) // BLOCK

    def factor_of(which):
        factor = fac_ref[0, 0, 0:1, which * features:(which + 1) * features]
        full = jnp.broadcast_to(factor, (cells, features))
        for at in range(1, breadth // BLOCK):
            factor = fac_ref[0, 0, at:at + 1, which * features:(which + 1) * features]
            full = jnp.where(block_col == at, factor, full)
        return full

    q_out[0] = (q_ref[0].astype(F32) * factor_of(0)).astype(BF16)
    kv_out[0, 0] = (k_ref[0].astype(F32) * factor_of(1)).astype(BF16)
    kv_out[1, 0] = (v_ref[0].astype(F32) * factor_of(2)).astype(BF16)
    row = lax.axis_index("row") * height + strip * BLOCK + cell // breadth
    col = lax.axis_index("col") * breadth + cell % breadth
    inside = (row >= crop_ref[frame, 0]) & (col >= crop_ref[frame, 1])
    masked = jnp.where(inside, g_ref[0].astype(F32), 0.0).astype(BF16)
    g_out[0] = masked
    do_out[0] = dot(masked, w_ref[...], ((1,), (1,))).astype(BF16)


def prepare(q, k, v, g, factors, crop_start, w_out, breadth):
    members, cells, features = q.shape
    strip_cells = BLOCK * breadth
    strips = cells // strip_cells
    spec = pl.BlockSpec((1, strip_cells, features), lambda b, t: (b, t, 0))
    kv_spec = pl.BlockSpec((2, 1, strip_cells, features), lambda b, t: (0, b, t, 0))
    shape = jax.ShapeDtypeStruct(q.shape, BF16)
    return pl.pallas_call(
        functools.partial(prepare_kernel, breadth=breadth),
        grid=(members, strips),
        in_specs=[spec, spec, spec, spec,
                  pl.BlockSpec((1, 1) + factors.shape[2:], lambda b, t: (b, t, 0, 0)),
                  pl.BlockSpec(memory_space=pltpu.SMEM),
                  pl.BlockSpec(w_out.shape, lambda b, t: (0, 0))],
        out_specs=[spec, kv_spec, spec, spec],
        out_shape=[shape, jax.ShapeDtypeStruct((2,) + q.shape, BF16), shape, shape],
        name="prepare",
    )(q, k, v, g, factors, crop_start, w_out)


def attend_kernel(q_ref, do_ref, kvc_ref, kvs_ref, ot_ref, dq_ref, dc_ref, ds_ref, bias_ref,
                  *, breadth, head_dim):
    strip_cells = BLOCK * breadth
    side_cells = BLOCK * 2 * RADIUS
    strips = q_ref.shape[1] // strip_cells
    keys_c, keys_s = 2 * strip_cells, 2 * side_cells
    keys = keys_c + keys_s
    lanes = q_ref.shape[2]
    stacked = (lanes // head_dim) * strip_cells
    height = strips * BLOCK

    @pl.when((pl.program_id(0) == 0) & (pl.program_id(1) == 0))
    def _():
        key = lax.broadcasted_iota(jnp.int32, (keys, stacked), 0)
        query = lax.broadcasted_iota(jnp.int32, (keys, stacked), 1) % strip_cells
        side = key - keys_c
        key_row = jnp.where(key < keys_c, key // breadth, side // (2 * RADIUS)) - RADIUS
        along = side % (2 * RADIUS)
        key_col = jnp.where(
            key < keys_c, key % breadth,
            jnp.where(along < RADIUS, along - RADIUS, along - RADIUS + breadth))
        d_row = key_row - query // breadth
        d_col = key_col - query % breadth
        near = (jnp.abs(d_row) <= RADIUS) & (jnp.abs(d_col) <= RADIUS)
        frame_rows = height * lax.axis_size("row")
        frame_cols = breadth * lax.axis_size("col")
        at_col = key_col + lax.axis_index("col") * breadth
        near = near & (at_col >= 0) & (at_col < frame_cols)
        for strip in range(strips):
            at_row = key_row + strip * BLOCK + lax.axis_index("row") * height
            seen = near & (at_row >= 0) & (at_row < frame_rows)
            bias_ref[strip] = jnp.where(seen, 0.0, masked_score)

    lane = lax.broadcasted_iota(jnp.int32, (strip_cells, lanes), 1)
    masks = [jnp.where(lane // head_dim == h, 1.0, 0.0).astype(BF16)
             for h in range(lanes // head_dim)]
    scale = 1.0 / math.sqrt(head_dim)

    def by_head(whole):
        return jnp.concatenate(
            [whole[h * head_dim:(h + 1) * head_dim, h * strip_cells:(h + 1) * strip_cells]
             for h in range(lanes // head_dim)], 0)

    carry = None
    for strip in range(strips):
        at = slice(strip * strip_cells, (strip + 1) * strip_cells)
        at_c = slice(strip * strip_cells, strip * strip_cells + keys_c)
        at_s = slice(strip * side_cells, strip * side_cells + keys_s)
        q = q_ref[0, at] * scale
        g = do_ref[0, at]
        q_stack = jnp.concatenate([q * m for m in masks], 0)
        g_stack = jnp.concatenate([g * m for m in masks], 0)
        k = jnp.concatenate([kvc_ref[0, 0, at_c], kvs_ref[0, 0, at_s]], 0)
        v = jnp.concatenate([kvc_ref[1, 0, at_c], kvs_ref[1, 0, at_s]], 0)
        scores = dot(k, q_stack, ((1,), (1,))) + bias_ref[strip]
        weights = jnp.exp(scores - jnp.max(scores, axis=0, keepdims=True))
        softmax = weights * (1.0 / jnp.sum(weights, axis=0, keepdims=True))
        half = softmax.astype(BF16)
        grad_probs = dot(v, g_stack, ((1,), (1,)))
        delta = jnp.sum(softmax * grad_probs, axis=0, keepdims=True)
        grad_scores = (softmax * (grad_probs - delta)).astype(BF16)
        ot_ref[:, at] = by_head(dot(v, half, ((0,), (0,)))).astype(BF16)
        dq = by_head(dot(k, grad_scores, ((0,), (0,)))) * scale
        dq_ref[0, at] = dq.T.astype(BF16)
        parts = (dot(grad_scores, q_stack, ((1,), (0,))), dot(half, g_stack, ((1,), (0,))))
        for which in range(2):
            part_c, part_s = parts[which][:keys_c], parts[which][keys_c:]
            first_c, first_s = part_c[:strip_cells], part_s[:side_cells]
            if carry is not None:
                first_c = first_c + carry[which][0]
                first_s = first_s + carry[which][1]
            dc_ref[which, 0, at] = first_c
            ds_ref[which, 0, strip * side_cells:(strip + 1) * side_cells] = first_s.astype(BF16)
        carry = [(p[strip_cells:keys_c], p[keys_c + side_cells:]) for p in parts]
    for which in range(2):
        dc_ref[which, 0, strips * strip_cells:] = carry[which][0]
        ds_ref[which, 0, strips * side_cells:] = carry[which][1].astype(BF16)


def attend(q, do, kv_c, kv_s, breadth):
    members, cells, features = q.shape
    head_dim = features // HEADS
    lanes = 128
    strips = cells // (BLOCK * breadth)
    keys = 2 * BLOCK * (breadth + 2 * RADIUS)
    stacked = (lanes // head_dim) * BLOCK * breadth
    spec = pl.BlockSpec((1, cells, lanes), lambda b, h: (b, 0, h))

    def kv_spec(array):
        return pl.BlockSpec((2, 1, array.shape[2], lanes), lambda b, h: (0, b, 0, h))

    return pl.pallas_call(
        functools.partial(attend_kernel, breadth=breadth, head_dim=head_dim),
        grid=(members, features // lanes),
        in_specs=[spec, spec, kv_spec(kv_c), kv_spec(kv_s)],
        out_specs=[pl.BlockSpec((lanes, cells), lambda b, h: (h, b)), spec,
                   kv_spec(kv_c), kv_spec(kv_s)],
        out_shape=[jax.ShapeDtypeStruct((features, members * cells), BF16),
                   jax.ShapeDtypeStruct(q.shape, BF16),
                   jax.ShapeDtypeStruct(kv_c.shape, F32),
                   jax.ShapeDtypeStruct(kv_s.shape, BF16)],
        scratch_shapes=[pltpu.VMEM((strips, keys, stacked), F32)],
        name="attend",
    )(q, do, kv_c, kv_s)


def bits_of(count):
    return max(count.bit_length() - 1, 0)


def halving_orders(rows, cols):
    col = [("col", k) for k in range(bits_of(cols))]
    row = [("row", k) for k in range(bits_of(rows))]
    return [col[:1] + col[1:] + row, col[:1] + col[:0:-1] + row]


def col_place(order, col):
    place = 0
    for axis, bit in order:
        if axis == "col":
            place = 2 * place + (col >> bit) % 2
    return place


def weights_kernel(tok_ref, ot_ref, dq_ref, dk_ref, dv_ref, g_ref, w_ref,
                   dq_rows, dk_rows, dv_rows, gt_ref, buf_ref, *, orders, rows, cols):
    features = g_ref.shape[1]
    tok = tok_ref[...]
    raw = jnp.concatenate(
        [dot(tok, ref[...], ((0,), (0,))) for ref in (dq_ref, dk_ref, dv_ref)], 1)
    raw_out = dot(ot_ref[...], g_ref[...], ((1,), (0,)))
    wide, narrow = 3 * features // cols, features // cols
    part_rows = buf_ref.shape[3]
    group = tok.shape[1] // (2 * part_rows)
    nbits = bits_of(rows)
    for member, col in ((m, c) for m in range(group) for c in range(cols)):
        row = pl.program_id(0) * group + member
        place = sum(((row // 2 ** k) % 2) * 2 ** (nbits - 1 - k) for k in range(nbits))
        piece = jnp.concatenate(
            [raw[:, col * wide:(col + 1) * wide], raw_out[:, col * narrow:(col + 1) * narrow]],
            1).astype(BF16)
        for half, order in enumerate(orders):
            first = (2 * member + half) * part_rows
            buf_ref[half, col_place(order, col), place] = piece[first:first + part_rows]
    total = dot(dq_rows[...], w_ref[:, :features], ((1,), (1,)))
    total = total + dot(dk_rows[...], w_ref[:, features:2 * features], ((1,), (1,)))
    total = total + dot(dv_rows[...], w_ref[:, 2 * features:], ((1,), (1,)))
    gt_ref[...] = total.astype(BF16)


def weight_pieces(tokens, o_t, dq, dk, dv, g, w_qkv, rows, cols):
    cells, features = tokens.shape
    orders = halving_orders(rows, cols)
    part_rows = features // rows
    group = max(1, 128 // part_rows)
    whole = pl.BlockSpec((cells, features), lambda r: (0, 0))
    some = pl.BlockSpec((cells * group // rows, features), lambda r: (r, 0))
    lanes = 4 * features // cols
    return pl.pallas_call(
        functools.partial(weights_kernel, orders=orders, rows=rows, cols=cols),
        grid=(rows // group,),
        in_specs=[pl.BlockSpec((cells, group * part_rows), lambda r: (0, r)),
                  pl.BlockSpec((group * part_rows, cells), lambda r: (r, 0)),
                  whole, whole, whole, whole,
                  pl.BlockSpec(w_qkv.shape, lambda r: (0, 0)), some, some, some],
        out_specs=[some, pl.BlockSpec((2, cols, rows, part_rows // 2, lanes),
                                      lambda r: (0, 0, 0, 0, 0))],
        out_shape=[jax.ShapeDtypeStruct((cells, features), BF16),
                   jax.ShapeDtypeStruct((2, cols, rows, part_rows // 2, lanes), BF16)],
        name="weights",
    )(tokens, o_t, dq, dk, dv, g, w_qkv, dq, dk, dv)


def reduce_kernel(buf_ref, qkv_ref, out_ref, work, recv, own_sq, all_sq,
                  send_sem, recv_sem, sq_send, sq_recv, *, rows, cols):
    orders = halving_orders(rows, cols)
    count = rows * cols
    mine = {"row": lax.axis_index("row"), "col": lax.axis_index("col")}
    me = mine["row"] * cols + mine["col"]

    def other(i):
        at = lax.rem(me + i, count)
        return (at // cols, at % cols)

    barrier = pltpu.get_barrier_semaphore()

    def greet(i, _):
        pl.semaphore_signal(barrier, inc=1, device_id=other(i),
                            device_id_type=pl.DeviceIdType.MESH)
        return 0

    lax.fori_loop(1, count, greet, 0)
    pl.semaphore_wait(barrier, count - 1)
    steps = len(orders[0])
    base = [0, 0]
    finals = [None, None]

    def start(half, step):
        axis, bit = orders[half][step]
        size = count >> (step + 1)
        mybit = (mine[axis] // 2 ** bit) % 2
        partner = dict(mine)
        partner[axis] = mine[axis] + (1 - 2 * mybit) * 2 ** bit
        source = buf_ref if step == 0 else work
        at = recv.at[half, pl.ds(count - 2 * size, size)]
        copy = pltpu.make_async_remote_copy(
            src_ref=source.at[half, pl.ds(base[half] + (1 - mybit) * size, size)],
            dst_ref=at, send_sem=send_sem.at[half, step], recv_sem=recv_sem.at[half, step],
            device_id=(partner["row"], partner["col"]),
            device_id_type=pl.DeviceIdType.MESH)
        copy.start()
        return copy, size, mybit

    flights = [start(half, 0) for half in range(2)]
    for step in range(steps):
        for half in range(2):
            copy, size, mybit = flights[half]
            copy.wait()
            keep = base[half] + mybit * size
            first = count - 2 * size
            if step == steps - 1:
                finals[half] = work[half, keep].astype(F32) + recv[half, first].astype(F32)
                continue
            source = buf_ref if step == 0 else work
            base[half] = 0 if step == 0 else keep

            def add(i, _, half=half, keep=keep, first=first, source=source, to=base[half]):
                work[half, to + i] = (source[half, keep + i].astype(F32)
                                      + recv[half, first + i].astype(F32)).astype(BF16)
                return 0

            lax.fori_loop(0, size, add, 0)
            flights[half] = start(half, step + 1)
    part = jnp.concatenate(finals, 0)
    squares = jnp.sum((part * part).reshape(-1, 8, part.shape[1]), axis=0)
    tile = own_sq.shape[1]
    own_sq[...] = sum(squares[:, j * tile:(j + 1) * tile] for j in range(part.shape[1] // tile))

    def square_copy(i):
        return pltpu.make_async_remote_copy(
            src_ref=own_sq, dst_ref=all_sq.at[i], send_sem=sq_send.at[i],
            recv_sem=sq_recv.at[i], device_id=other(i),
            device_id_type=pl.DeviceIdType.MESH)

    def send(i, _):
        square_copy(i).start()
        return 0

    def take(i, total):
        square_copy(i).wait()
        return total + all_sq[i]

    lax.fori_loop(1, count, send, 0)
    total = jnp.sum(lax.fori_loop(1, count, take, own_sq[...]), keepdims=True)
    factor = jnp.minimum(1.0, max_norm / jnp.sqrt(total + tiny_square))
    part = part * factor
    split = qkv_ref.shape[1]
    qkv_ref[...] = part[:, :split]
    out_ref[...] = part[:, split:]


def reduce_pieces(pieces, rows, cols):
    count = rows * cols
    half_rows, lanes = pieces.shape[3:]
    pieces = pieces.reshape(2, count, half_rows, lanes)
    steps = bits_of(count)
    vmem = pl.BlockSpec(memory_space=pltpu.VMEM)
    return pl.pallas_call(
        functools.partial(reduce_kernel, rows=rows, cols=cols),
        in_specs=[vmem], out_specs=[vmem, vmem],
        out_shape=[jax.ShapeDtypeStruct((2 * half_rows, 3 * lanes // 4), F32),
                   jax.ShapeDtypeStruct((2 * half_rows, lanes // 4), F32)],
        scratch_shapes=[
            pltpu.VMEM((2, count // 2, half_rows, lanes), BF16),
            pltpu.VMEM((2, count, half_rows, lanes), BF16),
            pltpu.VMEM((8, 128), F32), pltpu.VMEM((count, 8, 128), F32),
            pltpu.SemaphoreType.DMA((2, steps)), pltpu.SemaphoreType.DMA((2, steps)),
            pltpu.SemaphoreType.DMA((count,)), pltpu.SemaphoreType.DMA((count,))],
        compiler_params=pltpu.CompilerParams(collective_id=1, has_side_effects=True),
        name="reduce",
    )(pieces)


def passed_along(array, axis, by):
    size = lax.axis_size(axis)
    return lax.ppermute(
        array, axis, [(i, i + by) for i in range(size) if 0 <= i + by < size])


def body(tokens, w_qkv, w_out, q_saved, k_saved, v_saved, scale_exp, grad_out, crop_start):
    members, height, breadth, features = tokens.shape
    cells = height * breadth
    rows, cols = lax.axis_size("row"), lax.axis_size("col")
    factors = jnp.repeat(jnp.exp2(scale_exp.astype(F32)), features // HEADS, axis=3)

    def flat(array):
        return array.reshape(members, cells, features)

    q, kv, g, do = prepare(flat(q_saved), flat(k_saved), flat(v_saved), flat(grad_out),
                           factors, crop_start, w_out, breadth)
    edge = RADIUS * breadth
    kv_c = jnp.concatenate(
        [passed_along(kv[:, :, -edge:], "row", 1), kv,
         passed_along(kv[:, :, :edge], "row", -1)], axis=2)
    grid = kv_c.reshape(2, members, height + 2 * RADIUS, breadth, features)
    kv_s = jnp.concatenate(
        [passed_along(grid[:, :, :, -RADIUS:], "col", 1),
         passed_along(grid[:, :, :, :RADIUS], "col", -1)], axis=3)
    kv_s = kv_s.reshape(2, members, -1, features)
    o_t, dq, d_c, d_s = attend(q, do, kv_c, kv_s, breadth)
    d_c = d_c.reshape(2, members, height + 2 * RADIUS, breadth, features)
    d_s = d_s.reshape(2, members, height + 2 * RADIUS, 2 * RADIUS, features)
    from_left = passed_along(d_s[:, :, :, RADIUS:], "col", 1)
    from_right = passed_along(d_s[:, :, :, :RADIUS], "col", -1)
    gap = jnp.zeros(d_s.shape[:3] + (breadth - 2 * RADIUS, features), BF16)
    d_c = d_c + jnp.concatenate([from_left, gap, from_right], axis=3).astype(F32)
    from_up = passed_along(d_c[:, :, -RADIUS:].astype(BF16), "row", 1)
    from_down = passed_along(d_c[:, :, :RADIUS].astype(BF16), "row", -1)
    gap = jnp.zeros((2, members, height - 2 * RADIUS, breadth, features), BF16)
    owned = d_c[:, :, RADIUS:-RADIUS] + jnp.concatenate(
        [from_up, gap, from_down], axis=2).astype(F32)
    owned = owned.astype(BF16).reshape(2, members * cells, features)
    grad_tokens, pieces = weight_pieces(
        tokens.reshape(-1, features), o_t, dq.reshape(-1, features), owned[0], owned[1],
        g.reshape(-1, features), w_qkv, rows, cols)
    grad_qkv, grad_out_w = reduce_pieces(pieces, rows, cols)
    return grad_tokens.reshape(tokens.shape), grad_qkv, grad_out_w


def solution(mesh):
    placed = (
        P(None, "row", "col", None), P(), P(),
        P(None, "row", "col", None), P(None, "row", "col", None),
        P(None, "row", "col", None), P(None, "row", "col", None),
        P(None, "row", "col", None), P(),
    )
    return jax.shard_map(
        body, mesh=mesh, in_specs=placed,
        out_specs=(P(None, "row", "col", None), P("row", "col"), P("row", "col")),
        check_vma=False)
```

```python
import functools
import math

import jax
import jax.numpy as jnp
from jax import lax
from jax.experimental import pallas as pl
from jax.experimental.pallas import tpu as pltpu
from jax.sharding import PartitionSpec as P

HEADS = 8
RADIUS = 4
BLOCK = 8

max_norm = 1000.0
masked_score = -1e30
tiny_square = 1e-06
F32 = jnp.float32
BF16 = jnp.bfloat16


def dot(left, right, dims):
    return lax.dot_general(left, right, (dims, ((), ())), preferred_element_type=F32)


def prepare_kernel(q_ref, k_ref, v_ref, g_ref, fac_ref, crop_ref, w_ref,
                   q_out, kv_out, g_out, do_out, *, breadth):
    frame = pl.program_id(0)
    strip = pl.program_id(1)
    cells, features = q_ref.shape[1:]
    height = BLOCK * pl.num_programs(1)
    cell = lax.broadcasted_iota(jnp.int32, (cells, features), 0)
    block_col = (cell % breadth) // BLOCK

    def factor_of(which):
        factor = fac_ref[0, 0, 0:1, which * features:(which + 1) * features]
        full = jnp.broadcast_to(factor, (cells, features))
        for at in range(1, breadth // BLOCK):
            factor = fac_ref[0, 0, at:at + 1, which * features:(which + 1) * features]
            full = jnp.where(block_col == at, factor, full)
        return full

    q_out[0] = (q_ref[0].astype(F32) * factor_of(0)).astype(BF16)
    kv_out[0, 0] = (k_ref[0].astype(F32) * factor_of(1)).astype(BF16)
    kv_out[1, 0] = (v_ref[0].astype(F32) * factor_of(2)).astype(BF16)
    row = lax.axis_index("row") * height + strip * BLOCK + cell // breadth
    col = lax.axis_index("col") * breadth + cell % breadth
    inside = (row >= crop_ref[frame, 0]) & (col >= crop_ref[frame, 1])
    masked = jnp.where(inside, g_ref[0].astype(F32), 0.0).astype(BF16)
    g_out[0] = masked
    do_out[0] = dot(masked, w_ref[...], ((1,), (1,))).astype(BF16)


def prepare(q, k, v, g, factors, crop_start, w_out, breadth):
    members, cells, features = q.shape
    strip_cells = BLOCK * breadth
    strips = cells // strip_cells
    spec = pl.BlockSpec((1, strip_cells, features), lambda b, t: (b, t, 0))
    kv_spec = pl.BlockSpec((2, 1, strip_cells, features), lambda b, t: (0, b, t, 0))
    shape = jax.ShapeDtypeStruct(q.shape, BF16)
    return pl.pallas_call(
        functools.partial(prepare_kernel, breadth=breadth),
        grid=(members, strips),
        in_specs=[spec, spec, spec, spec,
                  pl.BlockSpec((1, 1) + factors.shape[2:], lambda b, t: (b, t, 0, 0)),
                  pl.BlockSpec(memory_space=pltpu.SMEM),
                  pl.BlockSpec(w_out.shape, lambda b, t: (0, 0))],
        out_specs=[spec, kv_spec, spec, spec],
        out_shape=[shape, jax.ShapeDtypeStruct((2,) + q.shape, BF16), shape, shape],
        name="prepare",
    )(q, k, v, g, factors, crop_start, w_out)


def attend_kernel(q_ref, do_ref, kv_ref, rows_ref, sides_ref, ot_ref, dq_ref, own_ref,
                  drows_ref, dsides_ref, bias_ref, *, breadth, head_dim):
    strip_cells = BLOCK * breadth
    rim_c = RADIUS * breadth
    side_cells = BLOCK * RADIUS
    cells = q_ref.shape[1]
    strips = cells // strip_cells
    keys_c, keys_s = 2 * strip_cells, 2 * side_cells
    keys = keys_c + 2 * keys_s
    lanes = q_ref.shape[2]
    stacked = (lanes // head_dim) * strip_cells
    height = strips * BLOCK

    @pl.when((pl.program_id(0) == 0) & (pl.program_id(1) == 0))
    def _():
        key = lax.broadcasted_iota(jnp.int32, (keys, stacked), 0)
        query = lax.broadcasted_iota(jnp.int32, (keys, stacked), 1) % strip_cells
        side = key - keys_c
        key_row = jnp.where(key < keys_c, key // breadth, (side % keys_s) // RADIUS) - RADIUS
        key_col = jnp.where(
            key < keys_c, key % breadth,
            side % RADIUS + jnp.where(side < keys_s, -RADIUS, breadth))
        d_row = key_row - query // breadth
        d_col = key_col - query % breadth
        near = (jnp.abs(d_row) <= RADIUS) & (jnp.abs(d_col) <= RADIUS)
        frame_rows = height * lax.axis_size("row")
        frame_cols = breadth * lax.axis_size("col")
        at_col = key_col + lax.axis_index("col") * breadth
        near = near & (at_col >= 0) & (at_col < frame_cols)
        for strip in range(strips):
            at_row = key_row + strip * BLOCK + lax.axis_index("row") * height
            seen = near & (at_row >= 0) & (at_row < frame_rows)
            bias_ref[strip] = jnp.where(seen, 0.0, masked_score)

    lane = lax.broadcasted_iota(jnp.int32, (strip_cells, lanes), 1)
    masks = [jnp.where(lane // head_dim == h, 1.0, 0.0).astype(BF16)
             for h in range(lanes // head_dim)]
    scale = 1.0 / math.sqrt(head_dim)

    def by_head(whole):
        return jnp.concatenate(
            [whole[h * head_dim:(h + 1) * head_dim, h * strip_cells:(h + 1) * strip_cells]
             for h in range(lanes // head_dim)], 0)

    def keys_of(which, strip):
        low, high = strip * strip_cells - rim_c, (strip + 2) * strip_cells - rim_c
        parts = [kv_ref[which, 0, max(low, 0):min(high, cells)]]
        if low < 0:
            parts.insert(0, rows_ref[0, which, 0])
        if high > cells:
            parts.append(rows_ref[1, which, 0])
        for side in range(2):
            parts.append(sides_ref[side, which, 0, strip * side_cells:strip * side_cells + keys_s])
        return jnp.concatenate(parts, 0)

    def put(which, chunk, center, sides):
        low = chunk * strip_cells - rim_c
        if chunk == 0:
            drows_ref[0, which, 0] = center[:rim_c].astype(BF16)
            own_ref[which, 0, :strip_cells - rim_c] = center[rim_c:]
        elif chunk == strips:
            own_ref[which, 0, low:] = center[:cells - low]
            drows_ref[1, which, 0] = center[cells - low:].astype(BF16)
        else:
            own_ref[which, 0, low:low + strip_cells] = center
        for side in range(2):
            dsides_ref[side, which, 0, chunk * side_cells:(chunk + 1) * side_cells] = (
                sides[side].astype(BF16))

    carry = None
    for strip in range(strips):
        at = slice(strip * strip_cells, (strip + 1) * strip_cells)
        q = q_ref[0, at] * scale
        g = do_ref[0, at]
        q_stack = jnp.concatenate([q * m for m in masks], 0)
        g_stack = jnp.concatenate([g * m for m in masks], 0)
        k, v = keys_of(0, strip), keys_of(1, strip)
        scores = dot(k, q_stack, ((1,), (1,))) + bias_ref[strip]
        weights = jnp.exp(scores - jnp.max(scores, axis=0, keepdims=True))
        softmax = weights * (1.0 / jnp.sum(weights, axis=0, keepdims=True))
        half = softmax.astype(BF16)
        grad_probs = dot(v, g_stack, ((1,), (1,)))
        delta = jnp.sum(softmax * grad_probs, axis=0, keepdims=True)
        grad_scores = (softmax * (grad_probs - delta)).astype(BF16)
        ot_ref[:, at] = by_head(dot(v, half, ((0,), (0,)))).astype(BF16)
        dq = by_head(dot(k, grad_scores, ((0,), (0,)))) * scale
        dq_ref[0, at] = dq.T.astype(BF16)
        parts = (dot(grad_scores, q_stack, ((1,), (0,))), dot(half, g_stack, ((1,), (0,))))
        after = []
        for which in range(2):
            pieces = [parts[which][:strip_cells]]
            rest = [parts[which][strip_cells:keys_c]]
            for side in range(2):
                first = keys_c + side * keys_s
                pieces.append(parts[which][first:first + side_cells])
                rest.append(parts[which][first + side_cells:first + keys_s])
            if carry is not None:
                pieces = [p + c for p, c in zip(pieces, carry[which])]
            put(which, strip, pieces[0], pieces[1:])
            after.append(rest)
        carry = after
    for which in range(2):
        put(which, strips, carry[which][0], carry[which][1:])


def attend(q, do, kv, rim_rows, sides, breadth):
    members, cells, features = q.shape
    head_dim = features // HEADS
    lanes = 128
    strips = cells // (BLOCK * breadth)
    keys = 2 * BLOCK * (breadth + 2 * RADIUS)
    stacked = (lanes // head_dim) * BLOCK * breadth
    spec = pl.BlockSpec((1, cells, lanes), lambda b, h: (b, 0, h))

    def kv_spec(array):
        lead = array.shape[:-3]
        return pl.BlockSpec(lead + (1, array.shape[-2], lanes),
                            lambda b, h: (0,) * len(lead) + (b, 0, h))

    return pl.pallas_call(
        functools.partial(attend_kernel, breadth=breadth, head_dim=head_dim),
        grid=(members, features // lanes),
        in_specs=[spec, spec, kv_spec(kv), kv_spec(rim_rows), kv_spec(sides)],
        out_specs=[pl.BlockSpec((lanes, cells), lambda b, h: (h, b)), spec,
                   kv_spec(kv), kv_spec(rim_rows), kv_spec(sides)],
        out_shape=[jax.ShapeDtypeStruct((features, members * cells), BF16),
                   jax.ShapeDtypeStruct(q.shape, BF16),
                   jax.ShapeDtypeStruct(kv.shape, F32),
                   jax.ShapeDtypeStruct(rim_rows.shape, BF16),
                   jax.ShapeDtypeStruct(sides.shape, BF16)],
        scratch_shapes=[pltpu.VMEM((strips, keys, stacked), F32)],
        name="attend",
    )(q, do, kv, rim_rows, sides)


DIRECTIONS = [(0, 1), (0, -1), (1, 0), (-1, 0), (1, 1), (1, -1), (-1, 1), (-1, -1)]


def exchange_kernel(*refs, rows, cols, inputs, table):
    arrays, (send_sem, recv_sem) = refs[:-2], refs[-2:]
    sources, targets = arrays[:inputs], arrays[inputs:]
    row, col = lax.axis_index("row"), lax.axis_index("col")

    def present(dr, dc):
        return ((row + dr >= 0) & (row + dr < rows) & (col + dc >= 0) & (col + dc < cols))

    barrier = pltpu.get_barrier_semaphore()
    met = 0
    for dr, dc in DIRECTIONS:
        there = present(dr, dc)

        @pl.when(there)
        def _(dr=dr, dc=dc):
            pl.semaphore_signal(barrier, inc=1, device_id=(row + dr, col + dc),
                                device_id_type=pl.DeviceIdType.MESH)

        met = met + there.astype(jnp.int32)
    pl.semaphore_wait(barrier, met)

    def copy_of(at):
        dr, dc = DIRECTIONS[at]
        source, source_at, target, target_at = table[dr, dc]
        return pltpu.make_async_remote_copy(
            src_ref=sources[source].at[source_at], dst_ref=targets[target].at[target_at],
            send_sem=send_sem.at[at], recv_sem=recv_sem.at[at],
            device_id=(row + dr, col + dc), device_id_type=pl.DeviceIdType.MESH)

    for at, (dr, dc) in enumerate(DIRECTIONS):
        @pl.when(present(dr, dc))
        def _(at=at):
            copy_of(at).start()

    for at, (dr, dc) in enumerate(DIRECTIONS):
        @pl.when(jnp.logical_not(present(-dr, -dc)))
        def _(at=at):
            _, _, target, target_at = table[DIRECTIONS[at]]
            view = targets[target].at[target_at]
            view[...] = jnp.zeros(view.shape, BF16)

    for at, (dr, dc) in enumerate(DIRECTIONS):
        @pl.when(present(dr, dc))
        def _(at=at):
            copy_of(at).wait_send()

        @pl.when(present(-dr, -dc))
        def _(at=at):
            copy_of(at).wait_recv()


def exchange(arrays, shapes, table, rows, cols, collective_id, name):
    return pl.pallas_call(
        functools.partial(exchange_kernel, rows=rows, cols=cols, inputs=len(arrays),
                          table=table),
        in_specs=[pl.BlockSpec(memory_space=pl.ANY)] * len(arrays),
        out_specs=[pl.BlockSpec(memory_space=pltpu.VMEM)] * len(shapes),
        out_shape=[jax.ShapeDtypeStruct(shape, BF16) for shape in shapes],
        scratch_shapes=[pltpu.SemaphoreType.DMA((8,)), pltpu.SemaphoreType.DMA((8,))],
        compiler_params=pltpu.CompilerParams(
            collective_id=collective_id, has_side_effects=True),
        name=name,
    )(*arrays)


def span(*lead, first=0, size):
    return lead + (slice(None), slice(None), pl.ds(first, size))


def key_halos(kv, edges, breadth, rows, cols):
    _, members, cells, features = kv.shape
    rim, corner, along = RADIUS * breadth, RADIUS * RADIUS, edges.shape[3]
    last = along - corner
    table = {
        (1, 0): (0, span(first=cells - rim, size=rim), 0, span(0, size=rim)),
        (-1, 0): (0, span(size=rim), 0, span(1, size=rim)),
        (0, 1): (1, span(1, size=along), 1, span(0, first=corner, size=along)),
        (0, -1): (1, span(0, size=along), 1, span(1, first=corner, size=along)),
        (1, 1): (1, span(1, first=last, size=corner), 1, span(0, size=corner)),
        (1, -1): (1, span(0, first=last, size=corner), 1, span(1, size=corner)),
        (-1, 1): (1, span(1, size=corner), 1, span(0, first=corner + along, size=corner)),
        (-1, -1): (1, span(0, size=corner), 1, span(1, first=corner + along, size=corner)),
    }
    shapes = [(2, 2, members, rim, features), (2, 2, members, along + 2 * corner, features)]
    return exchange([kv, edges], shapes, table, rows, cols, 2, "key_halos")


def returned_rims(d_rows, d_sides, rows, cols):
    _, _, members, rim, features = d_rows.shape
    corner = RADIUS * RADIUS
    along = d_sides.shape[3] - 2 * corner
    end = corner + along
    table = {
        (1, 0): (0, span(1, size=rim), 0, span(0, size=rim)),
        (-1, 0): (0, span(0, size=rim), 0, span(1, size=rim)),
        (0, 1): (1, span(1, first=corner, size=along), 1, span(0, size=along)),
        (0, -1): (1, span(0, first=corner, size=along), 1, span(1, size=along)),
        (1, 1): (1, span(1, first=end, size=corner), 2, span(0, 0, size=corner)),
        (1, -1): (1, span(0, first=end, size=corner), 2, span(1, 0, size=corner)),
        (-1, 1): (1, span(1, size=corner), 2, span(0, 1, size=corner)),
        (-1, -1): (1, span(0, size=corner), 2, span(1, 1, size=corner)),
    }
    shapes = [d_rows.shape, (2, 2, members, along, features),
              (2, 2, 2, members, corner, features)]
    return exchange([d_rows, d_sides], shapes, table, rows, cols, 3, "returned_rims")


def bits_of(count):
    return max(count.bit_length() - 1, 0)


def halving_orders(rows, cols):
    col = [("col", k) for k in range(bits_of(cols))]
    row = [("row", k) for k in range(bits_of(rows))]
    return [col[:1] + col[1:] + row, col[:1] + col[:0:-1] + row]


def col_place(order, col):
    place = 0
    for axis, bit in order:
        if axis == "col":
            place = 2 * place + (col >> bit) % 2
    return place


def weights_kernel(tok_ref, ot_ref, dq_ref, dk_ref, dv_ref, g_ref, w_ref,
                   dq_rows, dk_rows, dv_rows, gt_ref, buf_ref, *, orders, rows, cols):
    features = g_ref.shape[1]
    tok = tok_ref[...]
    raw = jnp.concatenate(
        [dot(tok, ref[...], ((0,), (0,))) for ref in (dq_ref, dk_ref, dv_ref)], 1)
    raw_out = dot(ot_ref[...], g_ref[...], ((1,), (0,)))
    wide, narrow = 3 * features // cols, features // cols
    part_rows = buf_ref.shape[3]
    group = tok.shape[1] // (2 * part_rows)
    nbits = bits_of(rows)
    for member, col in ((m, c) for m in range(group) for c in range(cols)):
        row = pl.program_id(0) * group + member
        place = sum(((row // 2 ** k) % 2) * 2 ** (nbits - 1 - k) for k in range(nbits))
        piece = jnp.concatenate(
            [raw[:, col * wide:(col + 1) * wide], raw_out[:, col * narrow:(col + 1) * narrow]],
            1).astype(BF16)
        for half, order in enumerate(orders):
            first = (2 * member + half) * part_rows
            buf_ref[half, col_place(order, col), place] = piece[first:first + part_rows]
    total = dot(dq_rows[...], w_ref[:, :features], ((1,), (1,)))
    total = total + dot(dk_rows[...], w_ref[:, features:2 * features], ((1,), (1,)))
    total = total + dot(dv_rows[...], w_ref[:, 2 * features:], ((1,), (1,)))
    gt_ref[...] = total.astype(BF16)


def weight_pieces(tokens, o_t, dq, dk, dv, g, w_qkv, rows, cols):
    cells, features = tokens.shape
    orders = halving_orders(rows, cols)
    part_rows = features // rows
    group = max(1, 128 // part_rows)
    whole = pl.BlockSpec((cells, features), lambda r: (0, 0))
    some = pl.BlockSpec((cells * group // rows, features), lambda r: (r, 0))
    lanes = 4 * features // cols
    return pl.pallas_call(
        functools.partial(weights_kernel, orders=orders, rows=rows, cols=cols),
        grid=(rows // group,),
        in_specs=[pl.BlockSpec((cells, group * part_rows), lambda r: (0, r)),
                  pl.BlockSpec((group * part_rows, cells), lambda r: (r, 0)),
                  whole, whole, whole, whole,
                  pl.BlockSpec(w_qkv.shape, lambda r: (0, 0)), some, some, some],
        out_specs=[some, pl.BlockSpec((2, cols, rows, part_rows // 2, lanes),
                                      lambda r: (0, 0, 0, 0, 0))],
        out_shape=[jax.ShapeDtypeStruct((cells, features), BF16),
                   jax.ShapeDtypeStruct((2, cols, rows, part_rows // 2, lanes), BF16)],
        name="weights",
    )(tokens, o_t, dq, dk, dv, g, w_qkv, dq, dk, dv)


def reduce_kernel(buf_ref, part_ref, work, recv, own_sq, all_sq,
                  send_sem, recv_sem, sq_send, sq_recv, *, rows, cols):
    orders = halving_orders(rows, cols)
    count = rows * cols
    mine = {"row": lax.axis_index("row"), "col": lax.axis_index("col")}
    me = mine["row"] * cols + mine["col"]

    def other(i):
        at = lax.rem(me + i, count)
        return (at // cols, at % cols)

    barrier = pltpu.get_barrier_semaphore()

    def greet(i, _):
        pl.semaphore_signal(barrier, inc=1, device_id=other(i),
                            device_id_type=pl.DeviceIdType.MESH)
        return 0

    lax.fori_loop(1, count, greet, 0)
    pl.semaphore_wait(barrier, count - 1)
    steps = len(orders[0])
    base = [0, 0]
    finals = [None, None]

    def start(half, step):
        axis, bit = orders[half][step]
        size = count >> (step + 1)
        mybit = (mine[axis] // 2 ** bit) % 2
        partner = dict(mine)
        partner[axis] = mine[axis] + (1 - 2 * mybit) * 2 ** bit
        source = buf_ref if step == 0 else work
        at = recv.at[half, pl.ds(count - 2 * size, size)]
        copy = pltpu.make_async_remote_copy(
            src_ref=source.at[half, pl.ds(base[half] + (1 - mybit) * size, size)],
            dst_ref=at, send_sem=send_sem.at[half, step], recv_sem=recv_sem.at[half, step],
            device_id=(partner["row"], partner["col"]),
            device_id_type=pl.DeviceIdType.MESH)
        copy.start()
        return copy, size, mybit

    flights = [start(half, 0) for half in range(2)]
    for step in range(steps):
        for half in range(2):
            copy, size, mybit = flights[half]
            copy.wait()
            keep = base[half] + mybit * size
            first = count - 2 * size
            if step == steps - 1:
                finals[half] = work[half, keep].astype(F32) + recv[half, first].astype(F32)
                continue
            source = buf_ref if step == 0 else work
            base[half] = 0 if step == 0 else keep

            def add(i, _, half=half, keep=keep, first=first, source=source, to=base[half]):
                work[half, to + i] = (source[half, keep + i].astype(F32)
                                      + recv[half, first + i].astype(F32)).astype(BF16)
                return 0

            lax.fori_loop(0, size, add, 0)
            flights[half] = start(half, step + 1)
    part = jnp.concatenate(finals, 0)
    squares = jnp.sum((part * part).reshape(-1, 8, part.shape[1]), axis=0)
    tile = own_sq.shape[1]
    own_sq[...] = sum(squares[:, j * tile:(j + 1) * tile] for j in range(part.shape[1] // tile))

    def square_copy(i):
        return pltpu.make_async_remote_copy(
            src_ref=own_sq, dst_ref=all_sq.at[i], send_sem=sq_send.at[i],
            recv_sem=sq_recv.at[i], device_id=other(i),
            device_id_type=pl.DeviceIdType.MESH)

    def send(i, _):
        square_copy(i).start()
        return 0

    def take(i, total):
        square_copy(i).wait()
        return total + all_sq[i]

    lax.fori_loop(1, count, send, 0)
    total = jnp.sum(lax.fori_loop(1, count, take, own_sq[...]), keepdims=True)
    factor = jnp.minimum(1.0, max_norm / jnp.sqrt(total + tiny_square))
    part_ref[...] = part * factor


def reduce_pieces(pieces, rows, cols):
    count = rows * cols
    half_rows, lanes = pieces.shape[3:]
    pieces = pieces.reshape(2, count, half_rows, lanes)
    steps = bits_of(count)
    vmem = pl.BlockSpec(memory_space=pltpu.VMEM)
    return pl.pallas_call(
        functools.partial(reduce_kernel, rows=rows, cols=cols),
        in_specs=[vmem], out_specs=vmem,
        out_shape=jax.ShapeDtypeStruct((2 * half_rows, lanes), F32),
        scratch_shapes=[
            pltpu.VMEM((2, count // 2, half_rows, lanes), BF16),
            pltpu.VMEM((2, count, half_rows, lanes), BF16),
            pltpu.VMEM((8, 128), F32), pltpu.VMEM((count, 8, 128), F32),
            pltpu.SemaphoreType.DMA((2, steps)), pltpu.SemaphoreType.DMA((2, steps)),
            pltpu.SemaphoreType.DMA((count,)), pltpu.SemaphoreType.DMA((count,))],
        compiler_params=pltpu.CompilerParams(collective_id=1, has_side_effects=True),
        name="reduce",
    )(pieces)


def passed_along(array, axis, by):
    size = lax.axis_size(axis)
    return lax.ppermute(
        array, axis, [(i, i + by) for i in range(size) if 0 <= i + by < size])


def body(tokens, w_qkv, w_out, q_saved, k_saved, v_saved, scale_exp, grad_out, crop_start):
    members, height, breadth, features = tokens.shape
    cells = height * breadth
    rows, cols = lax.axis_size("row"), lax.axis_size("col")
    factors = jnp.repeat(jnp.exp2(scale_exp.astype(F32)), features // HEADS, axis=3)

    def flat(array):
        return array.reshape(members, cells, features)

    q, kv, g, do = prepare(flat(q_saved), flat(k_saved), flat(v_saved), flat(grad_out),
                           factors, crop_start, w_out, breadth)
    grid = kv.reshape(2, members, height, breadth, features)
    edges = jnp.stack([grid[:, :, :, :RADIUS], grid[:, :, :, -RADIUS:]])
    edges = edges.reshape(2, 2, members, height * RADIUS, features)
    rim_rows, sides = key_halos(kv, edges, breadth, rows, cols)
    o_t, dq, own, d_rows, d_sides = attend(q, do, kv, rim_rows, sides, breadth)
    rim_in, side_in, corner_in = returned_rims(d_rows, d_sides, rows, cols)
    gap = jnp.zeros((2, 2, members, (height - 2 * RADIUS) * RADIUS, features), BF16)
    side_in = side_in.astype(F32) + jnp.concatenate(
        [corner_in[:, 0], gap, corner_in[:, 1]], axis=3).astype(F32)
    side_in = side_in.reshape(2, 2, members, height, RADIUS, features)
    gap = jnp.zeros((2, members, height, breadth - 2 * RADIUS, features), F32)
    owned = own.reshape(grid.shape) + jnp.concatenate([side_in[0], gap, side_in[1]], axis=3)
    gap = jnp.zeros((2, members, cells - 2 * RADIUS * breadth, features), BF16)
    owned = owned.reshape(2, members, cells, features) + jnp.concatenate(
        [rim_in[0], gap, rim_in[1]], axis=2).astype(F32)
    owned = owned.astype(BF16).reshape(2, members * cells, features)
    grad_tokens, pieces = weight_pieces(
        tokens.reshape(-1, features), o_t, dq.reshape(-1, features), owned[0], owned[1],
        g.reshape(-1, features), w_qkv, rows, cols)
    part = reduce_pieces(pieces, rows, cols)
    split = 3 * features // cols
    return grad_tokens.reshape(tokens.shape), part[:, :split], part[:, split:]


def solution(mesh):
    placed = (
        P(None, "row", "col", None), P(), P(),
        P(None, "row", "col", None), P(None, "row", "col", None),
        P(None, "row", "col", None), P(None, "row", "col", None),
        P(None, "row", "col", None), P(),
    )
    return jax.shard_map(
        body, mesh=mesh, in_specs=placed,
        out_specs=(P(None, "row", "col", None), P("row", "col"), P("row", "col")),
        check_vma=False)
```

```python
import functools
import math

import jax
import jax.numpy as jnp
from jax import lax
from jax.experimental import pallas as pl
from jax.experimental.pallas import tpu as pltpu
from jax.sharding import PartitionSpec as P

HEADS = 8
RADIUS = 4
BLOCK = 8
PARTS = 4

max_norm = 1000.0
masked_score = -1e30
tiny_square = 1e-06
F32 = jnp.float32
BF16 = jnp.bfloat16


def dot(left, right, dims):
    return lax.dot_general(left, right, (dims, ((), ())), preferred_element_type=F32)


def prepare_kernel(q_ref, k_ref, v_ref, g_ref, fac_ref, crop_ref, w_ref,
                   q_out, kv_out, g_out, do_out, *, breadth):
    frame = pl.program_id(0)
    strip = pl.program_id(1)
    cells, features = q_ref.shape[1:]
    height = BLOCK * pl.num_programs(1)
    cell = lax.broadcasted_iota(jnp.int32, (cells, features), 0)
    block_col = (cell % breadth) // BLOCK

    def factor_of(which):
        factor = fac_ref[0, 0, 0:1, which * features:(which + 1) * features]
        full = jnp.broadcast_to(factor, (cells, features))
        for at in range(1, breadth // BLOCK):
            factor = fac_ref[0, 0, at:at + 1, which * features:(which + 1) * features]
            full = jnp.where(block_col == at, factor, full)
        return full

    q_out[0] = (q_ref[0].astype(F32) * factor_of(0)).astype(BF16)
    kv_out[0, 0] = (k_ref[0].astype(F32) * factor_of(1)).astype(BF16)
    kv_out[1, 0] = (v_ref[0].astype(F32) * factor_of(2)).astype(BF16)
    row = lax.axis_index("row") * height + strip * BLOCK + cell // breadth
    col = lax.axis_index("col") * breadth + cell % breadth
    inside = (row >= crop_ref[frame, 0]) & (col >= crop_ref[frame, 1])
    masked = jnp.where(inside, g_ref[0].astype(F32), 0.0).astype(BF16)
    g_out[0] = masked
    do_out[0] = dot(masked, w_ref[...], ((1,), (1,))).astype(BF16)


def prepare(q, k, v, g, factors, crop_start, w_out, breadth):
    members, cells, features = q.shape
    strip_cells = BLOCK * breadth
    strips = cells // strip_cells
    spec = pl.BlockSpec((1, strip_cells, features), lambda b, t: (b, t, 0))
    kv_spec = pl.BlockSpec((2, 1, strip_cells, features), lambda b, t: (0, b, t, 0))
    shape = jax.ShapeDtypeStruct(q.shape, BF16)
    return pl.pallas_call(
        functools.partial(prepare_kernel, breadth=breadth),
        grid=(members, strips),
        in_specs=[spec, spec, spec, spec,
                  pl.BlockSpec((1, 1) + factors.shape[2:], lambda b, t: (b, t, 0, 0)),
                  pl.BlockSpec(memory_space=pltpu.SMEM),
                  pl.BlockSpec(w_out.shape, lambda b, t: (0, 0))],
        out_specs=[spec, kv_spec, spec, spec],
        out_shape=[shape, jax.ShapeDtypeStruct((2,) + q.shape, BF16), shape, shape],
        name="prepare",
    )(q, k, v, g, factors, crop_start, w_out)


def attend_kernel(q_ref, do_ref, kv_ref, rows_ref, sides_ref, ot_ref, dq_ref, own_ref,
                  drows_ref, dsides_ref, bias_ref, *, breadth, head_dim):
    strip_cells = BLOCK * breadth
    rim_c = RADIUS * breadth
    side_cells = BLOCK * RADIUS
    cells = q_ref.shape[1]
    strips = cells // strip_cells
    keys_c, keys_s = 2 * strip_cells, 2 * side_cells
    keys = keys_c + 2 * keys_s
    lanes = q_ref.shape[2]
    stacked = (lanes // head_dim) * strip_cells
    height = strips * BLOCK

    @pl.when((pl.program_id(0) == 0) & (pl.program_id(1) == 0))
    def _():
        key = lax.broadcasted_iota(jnp.int32, (keys, stacked), 0)
        query = lax.broadcasted_iota(jnp.int32, (keys, stacked), 1) % strip_cells
        side = key - keys_c
        key_row = jnp.where(key < keys_c, key // breadth, (side % keys_s) // RADIUS) - RADIUS
        key_col = jnp.where(
            key < keys_c, key % breadth,
            side % RADIUS + jnp.where(side < keys_s, -RADIUS, breadth))
        d_row = key_row - query // breadth
        d_col = key_col - query % breadth
        near = (jnp.abs(d_row) <= RADIUS) & (jnp.abs(d_col) <= RADIUS)
        frame_rows = height * lax.axis_size("row")
        frame_cols = breadth * lax.axis_size("col")
        at_col = key_col + lax.axis_index("col") * breadth
        near = near & (at_col >= 0) & (at_col < frame_cols)
        for strip in range(strips):
            at_row = key_row + strip * BLOCK + lax.axis_index("row") * height
            seen = near & (at_row >= 0) & (at_row < frame_rows)
            bias_ref[strip] = jnp.where(seen, 0.0, masked_score)

    lane = lax.broadcasted_iota(jnp.int32, (strip_cells, lanes), 1)
    masks = [jnp.where(lane // head_dim == h, 1.0, 0.0).astype(BF16)
             for h in range(lanes // head_dim)]
    scale = 1.0 / math.sqrt(head_dim)

    def by_head(whole):
        return jnp.concatenate(
            [whole[h * head_dim:(h + 1) * head_dim, h * strip_cells:(h + 1) * strip_cells]
             for h in range(lanes // head_dim)], 0)

    def keys_of(which, strip):
        low, high = strip * strip_cells - rim_c, (strip + 2) * strip_cells - rim_c
        parts = [kv_ref[which, 0, max(low, 0):min(high, cells)]]
        if low < 0:
            parts.insert(0, rows_ref[0, which, 0])
        if high > cells:
            parts.append(rows_ref[1, which, 0])
        for side in range(2):
            parts.append(sides_ref[side, which, 0, strip * side_cells:strip * side_cells + keys_s])
        return jnp.concatenate(parts, 0)

    def put(which, chunk, center, sides):
        low = chunk * strip_cells - rim_c
        if chunk == 0:
            drows_ref[0, which, 0] = center[:rim_c].astype(BF16)
            own_ref[which, 0, :strip_cells - rim_c] = center[rim_c:]
        elif chunk == strips:
            own_ref[which, 0, low:] = center[:cells - low]
            drows_ref[1, which, 0] = center[cells - low:].astype(BF16)
        else:
            own_ref[which, 0, low:low + strip_cells] = center
        for side in range(2):
            dsides_ref[side, which, 0, chunk * side_cells:(chunk + 1) * side_cells] = (
                sides[side].astype(BF16))

    carry = None
    for strip in range(strips):
        at = slice(strip * strip_cells, (strip + 1) * strip_cells)
        q = q_ref[0, at] * scale
        g = do_ref[0, at]
        q_stack = jnp.concatenate([q * m for m in masks], 0)
        g_stack = jnp.concatenate([g * m for m in masks], 0)
        k, v = keys_of(0, strip), keys_of(1, strip)
        scores = dot(k, q_stack, ((1,), (1,))) + bias_ref[strip]
        weights = jnp.exp(scores - jnp.max(scores, axis=0, keepdims=True))
        softmax = weights * (1.0 / jnp.sum(weights, axis=0, keepdims=True))
        half = softmax.astype(BF16)
        grad_probs = dot(v, g_stack, ((1,), (1,)))
        delta = jnp.sum(softmax * grad_probs, axis=0, keepdims=True)
        grad_scores = (softmax * (grad_probs - delta)).astype(BF16)
        ot_ref[:, at] = by_head(dot(v, half, ((0,), (0,)))).astype(BF16)
        dq = by_head(dot(k, grad_scores, ((0,), (0,)))) * scale
        dq_ref[0, at] = dq.T.astype(BF16)
        parts = (dot(grad_scores, q_stack, ((1,), (0,))), dot(half, g_stack, ((1,), (0,))))
        after = []
        for which in range(2):
            pieces = [parts[which][:strip_cells]]
            rest = [parts[which][strip_cells:keys_c]]
            for side in range(2):
                first = keys_c + side * keys_s
                pieces.append(parts[which][first:first + side_cells])
                rest.append(parts[which][first + side_cells:first + keys_s])
            if carry is not None:
                pieces = [p + c for p, c in zip(pieces, carry[which])]
            put(which, strip, pieces[0], pieces[1:])
            after.append(rest)
        carry = after
    for which in range(2):
        put(which, strips, carry[which][0], carry[which][1:])


def attend(q, do, kv, rim_rows, sides, breadth):
    members, cells, features = q.shape
    head_dim = features // HEADS
    lanes = 128
    strips = cells // (BLOCK * breadth)
    keys = 2 * BLOCK * (breadth + 2 * RADIUS)
    stacked = (lanes // head_dim) * BLOCK * breadth
    spec = pl.BlockSpec((1, cells, lanes), lambda b, h: (b, 0, h))

    def kv_spec(array):
        lead = array.shape[:-3]
        return pl.BlockSpec(lead + (1, array.shape[-2], lanes),
                            lambda b, h: (0,) * len(lead) + (b, 0, h))

    return pl.pallas_call(
        functools.partial(attend_kernel, breadth=breadth, head_dim=head_dim),
        grid=(members, features // lanes),
        in_specs=[spec, spec, kv_spec(kv), kv_spec(rim_rows), kv_spec(sides)],
        out_specs=[pl.BlockSpec((lanes, cells), lambda b, h: (h, b)), spec,
                   kv_spec(kv), kv_spec(rim_rows), kv_spec(sides)],
        out_shape=[jax.ShapeDtypeStruct((features, members * cells), BF16),
                   jax.ShapeDtypeStruct(q.shape, BF16),
                   jax.ShapeDtypeStruct(kv.shape, F32),
                   jax.ShapeDtypeStruct(rim_rows.shape, BF16),
                   jax.ShapeDtypeStruct(sides.shape, BF16)],
        scratch_shapes=[pltpu.VMEM((strips, keys, stacked), F32)],
        name="attend",
    )(q, do, kv, rim_rows, sides)


DIRECTIONS = [(0, 1), (0, -1), (1, 0), (-1, 0), (1, 1), (1, -1), (-1, 1), (-1, -1)]


def exchange_kernel(*refs, rows, cols, inputs, table):
    arrays, (send_sem, recv_sem) = refs[:-2], refs[-2:]
    sources, targets = arrays[:inputs], arrays[inputs:]
    row, col = lax.axis_index("row"), lax.axis_index("col")

    def present(dr, dc):
        return ((row + dr >= 0) & (row + dr < rows) & (col + dc >= 0) & (col + dc < cols))

    barrier = pltpu.get_barrier_semaphore()
    met = 0
    for dr, dc in DIRECTIONS:
        there = present(dr, dc)

        @pl.when(there)
        def _(dr=dr, dc=dc):
            pl.semaphore_signal(barrier, inc=1, device_id=(row + dr, col + dc),
                                device_id_type=pl.DeviceIdType.MESH)

        met = met + there.astype(jnp.int32)
    pl.semaphore_wait(barrier, met)

    def copy_of(at):
        dr, dc = DIRECTIONS[at]
        source, source_at, target, target_at = table[dr, dc]
        return pltpu.make_async_remote_copy(
            src_ref=sources[source].at[source_at], dst_ref=targets[target].at[target_at],
            send_sem=send_sem.at[at], recv_sem=recv_sem.at[at],
            device_id=(row + dr, col + dc), device_id_type=pl.DeviceIdType.MESH)

    for at, (dr, dc) in enumerate(DIRECTIONS):
        @pl.when(present(dr, dc))
        def _(at=at):
            copy_of(at).start()

    for at, (dr, dc) in enumerate(DIRECTIONS):
        @pl.when(jnp.logical_not(present(-dr, -dc)))
        def _(at=at):
            _, _, target, target_at = table[DIRECTIONS[at]]
            view = targets[target].at[target_at]
            view[...] = jnp.zeros(view.shape, BF16)

    for at, (dr, dc) in enumerate(DIRECTIONS):
        @pl.when(present(dr, dc))
        def _(at=at):
            copy_of(at).wait_send()

        @pl.when(present(-dr, -dc))
        def _(at=at):
            copy_of(at).wait_recv()


def exchange(arrays, shapes, table, rows, cols, collective_id, name):
    return pl.pallas_call(
        functools.partial(exchange_kernel, rows=rows, cols=cols, inputs=len(arrays),
                          table=table),
        in_specs=[pl.BlockSpec(memory_space=pl.ANY)] * len(arrays),
        out_specs=[pl.BlockSpec(memory_space=pltpu.VMEM)] * len(shapes),
        out_shape=[jax.ShapeDtypeStruct(shape, BF16) for shape in shapes],
        scratch_shapes=[pltpu.SemaphoreType.DMA((8,)), pltpu.SemaphoreType.DMA((8,))],
        compiler_params=pltpu.CompilerParams(
            collective_id=collective_id, has_side_effects=True),
        name=name,
    )(*arrays)


def span(*lead, first=0, size):
    return lead + (slice(None), slice(None), pl.ds(first, size))


def key_halos(kv, edges, breadth, rows, cols):
    _, members, cells, features = kv.shape
    rim, corner, along = RADIUS * breadth, RADIUS * RADIUS, edges.shape[3]
    last = along - corner
    table = {
        (1, 0): (0, span(first=cells - rim, size=rim), 0, span(0, size=rim)),
        (-1, 0): (0, span(size=rim), 0, span(1, size=rim)),
        (0, 1): (1, span(1, size=along), 1, span(0, first=corner, size=along)),
        (0, -1): (1, span(0, size=along), 1, span(1, first=corner, size=along)),
        (1, 1): (1, span(1, first=last, size=corner), 1, span(0, size=corner)),
        (1, -1): (1, span(0, first=last, size=corner), 1, span(1, size=corner)),
        (-1, 1): (1, span(1, size=corner), 1, span(0, first=corner + along, size=corner)),
        (-1, -1): (1, span(0, size=corner), 1, span(1, first=corner + along, size=corner)),
    }
    shapes = [(2, 2, members, rim, features), (2, 2, members, along + 2 * corner, features)]
    return exchange([kv, edges], shapes, table, rows, cols, 2, "key_halos")


def returned_rims(d_rows, d_sides, rows, cols):
    _, _, members, rim, features = d_rows.shape
    corner = RADIUS * RADIUS
    along = d_sides.shape[3] - 2 * corner
    end = corner + along
    table = {
        (1, 0): (0, span(1, size=rim), 0, span(0, size=rim)),
        (-1, 0): (0, span(0, size=rim), 0, span(1, size=rim)),
        (0, 1): (1, span(1, first=corner, size=along), 1, span(0, size=along)),
        (0, -1): (1, span(0, first=corner, size=along), 1, span(1, size=along)),
        (1, 1): (1, span(1, first=end, size=corner), 2, span(0, 0, size=corner)),
        (1, -1): (1, span(0, first=end, size=corner), 2, span(1, 0, size=corner)),
        (-1, 1): (1, span(1, size=corner), 2, span(0, 1, size=corner)),
        (-1, -1): (1, span(0, size=corner), 2, span(1, 1, size=corner)),
    }
    shapes = [d_rows.shape, (2, 2, members, along, features),
              (2, 2, 2, members, corner, features)]
    return exchange([d_rows, d_sides], shapes, table, rows, cols, 3, "returned_rims")


def bits_of(count):
    return max(count.bit_length() - 1, 0)


def halving_orders(rows, cols):
    bits = [("col", k) for k in range(bits_of(cols))] + [("row", k) for k in range(bits_of(rows))]
    return [bits[k:] + bits[:k] for k in range(PARTS)]


def place_of(order, row, col):
    place = 0
    for axis, bit in order:
        place = 2 * place + ((row if axis == "row" else col) // 2 ** bit) % 2
    return place


def weights_kernel(tok_ref, ot_ref, dq_ref, dk_ref, dv_ref, g_ref, w_ref,
                   dq_rows, dk_rows, dv_rows, gt_ref, buf_ref, *, orders, cols):
    features = g_ref.shape[1]
    tok = tok_ref[...]
    raw = jnp.concatenate(
        [dot(tok, ref[...], ((0,), (0,))) for ref in (dq_ref, dk_ref, dv_ref)], 1)
    raw_out = dot(ot_ref[...], g_ref[...], ((1,), (0,)))
    wide, narrow = 3 * features // cols, features // cols
    part_rows = buf_ref.shape[2]
    group = tok.shape[1] // (PARTS * part_rows)
    for member, col in ((m, c) for m in range(group) for c in range(cols)):
        row = pl.program_id(0) * group + member
        piece = jnp.concatenate(
            [raw[:, col * wide:(col + 1) * wide], raw_out[:, col * narrow:(col + 1) * narrow]],
            1).astype(BF16)
        for half, order in enumerate(orders):
            first = (PARTS * member + half) * part_rows
            buf_ref[half, place_of(order, row, col)] = piece[first:first + part_rows]
    total = dot(dq_rows[...], w_ref[:, :features], ((1,), (1,)))
    total = total + dot(dk_rows[...], w_ref[:, features:2 * features], ((1,), (1,)))
    total = total + dot(dv_rows[...], w_ref[:, 2 * features:], ((1,), (1,)))
    gt_ref[...] = total.astype(BF16)


def weight_pieces(tokens, o_t, dq, dk, dv, g, w_qkv, rows, cols):
    cells, features = tokens.shape
    orders = halving_orders(rows, cols)
    part_rows = features // rows
    group = max(1, 128 // part_rows)
    whole = pl.BlockSpec((cells, features), lambda r: (0, 0))
    some = pl.BlockSpec((cells * group // rows, features), lambda r: (r, 0))
    lanes = 4 * features // cols
    return pl.pallas_call(
        functools.partial(weights_kernel, orders=orders, cols=cols),
        grid=(rows // group,),
        in_specs=[pl.BlockSpec((cells, group * part_rows), lambda r: (0, r)),
                  pl.BlockSpec((group * part_rows, cells), lambda r: (r, 0)),
                  whole, whole, whole, whole,
                  pl.BlockSpec(w_qkv.shape, lambda r: (0, 0)), some, some, some],
        out_specs=[some, pl.BlockSpec((PARTS, rows * cols, part_rows // PARTS, lanes),
                                      lambda r: (0, 0, 0, 0))],
        out_shape=[jax.ShapeDtypeStruct((cells, features), BF16),
                   jax.ShapeDtypeStruct((PARTS, rows * cols, part_rows // PARTS, lanes), BF16)],
        name="weights",
    )(tokens, o_t, dq, dk, dv, g, w_qkv, dq, dk, dv)


def reduce_kernel(buf_ref, part_ref, work, recv, own_sq, all_sq,
                  send_sem, recv_sem, sq_send, sq_recv, *, rows, cols):
    orders = halving_orders(rows, cols)
    count = rows * cols
    mine = {"row": lax.axis_index("row"), "col": lax.axis_index("col")}
    me = mine["row"] * cols + mine["col"]

    def other(i):
        at = lax.rem(me + i, count)
        return (at // cols, at % cols)

    barrier = pltpu.get_barrier_semaphore()

    def greet(i, _):
        pl.semaphore_signal(barrier, inc=1, device_id=other(i),
                            device_id_type=pl.DeviceIdType.MESH)
        return 0

    lax.fori_loop(1, count, greet, 0)
    pl.semaphore_wait(barrier, count - 1)
    steps = len(orders[0])
    base = [0] * PARTS
    finals = [None] * PARTS

    def start(half, step):
        axis, bit = orders[half][step]
        size = count >> (step + 1)
        mybit = (mine[axis] // 2 ** bit) % 2
        partner = dict(mine)
        partner[axis] = mine[axis] + (1 - 2 * mybit) * 2 ** bit
        source = buf_ref if step == 0 else work
        at = recv.at[half, pl.ds(count - 2 * size, size)]
        copy = pltpu.make_async_remote_copy(
            src_ref=source.at[half, pl.ds(base[half] + (1 - mybit) * size, size)],
            dst_ref=at, send_sem=send_sem.at[half, step], recv_sem=recv_sem.at[half, step],
            device_id=(partner["row"], partner["col"]),
            device_id_type=pl.DeviceIdType.MESH)
        copy.start()
        return copy, size, mybit

    flights = [start(half, 0) for half in range(PARTS)]
    for step in range(steps):
        for half in range(PARTS):
            copy, size, mybit = flights[half]
            copy.wait()
            keep = base[half] + mybit * size
            first = count - 2 * size
            if step == steps - 1:
                finals[half] = work[half, keep].astype(F32) + recv[half, first].astype(F32)
                continue
            source = buf_ref if step == 0 else work
            base[half] = 0 if step == 0 else keep

            work[half, pl.ds(base[half], size)] = (
                source[half, pl.ds(keep, size)] + recv[half, pl.ds(first, size)])
            flights[half] = start(half, step + 1)
    part = jnp.concatenate(finals, 0)
    squares = jnp.sum((part * part).reshape(-1, 8, part.shape[1]), axis=0)
    tile = own_sq.shape[1]
    own_sq[...] = sum(squares[:, j * tile:(j + 1) * tile] for j in range(part.shape[1] // tile))

    def square_copy(i):
        return pltpu.make_async_remote_copy(
            src_ref=own_sq, dst_ref=all_sq.at[i], send_sem=sq_send.at[i],
            recv_sem=sq_recv.at[i], device_id=other(i),
            device_id_type=pl.DeviceIdType.MESH)

    def send(i, _):
        square_copy(i).start()
        return 0

    def take(i, total):
        square_copy(i).wait()
        return total + all_sq[i]

    lax.fori_loop(1, count, send, 0)
    total = jnp.sum(lax.fori_loop(1, count, take, own_sq[...]), keepdims=True)
    factor = jnp.minimum(1.0, max_norm / jnp.sqrt(total + tiny_square))
    part_ref[...] = part * factor


def reduce_pieces(pieces, rows, cols):
    count = rows * cols
    half_rows, lanes = pieces.shape[2:]
    steps = bits_of(count)
    vmem = pl.BlockSpec(memory_space=pltpu.VMEM)
    return pl.pallas_call(
        functools.partial(reduce_kernel, rows=rows, cols=cols),
        in_specs=[vmem], out_specs=vmem,
        out_shape=jax.ShapeDtypeStruct((PARTS * half_rows, lanes), F32),
        scratch_shapes=[
            pltpu.VMEM((PARTS, count // 2, half_rows, lanes), BF16),
            pltpu.VMEM((PARTS, count, half_rows, lanes), BF16),
            pltpu.VMEM((8, 128), F32), pltpu.VMEM((count, 8, 128), F32),
            pltpu.SemaphoreType.DMA((PARTS, steps)),
            pltpu.SemaphoreType.DMA((PARTS, steps)),
            pltpu.SemaphoreType.DMA((count,)), pltpu.SemaphoreType.DMA((count,))],
        compiler_params=pltpu.CompilerParams(collective_id=1, has_side_effects=True),
        name="reduce",
    )(pieces)


def passed_along(array, axis, by):
    size = lax.axis_size(axis)
    return lax.ppermute(
        array, axis, [(i, i + by) for i in range(size) if 0 <= i + by < size])


def body(tokens, w_qkv, w_out, q_saved, k_saved, v_saved, scale_exp, grad_out, crop_start):
    members, height, breadth, features = tokens.shape
    cells = height * breadth
    rows, cols = lax.axis_size("row"), lax.axis_size("col")
    factors = jnp.repeat(jnp.exp2(scale_exp.astype(F32)), features // HEADS, axis=3)

    def flat(array):
        return array.reshape(members, cells, features)

    q, kv, g, do = prepare(flat(q_saved), flat(k_saved), flat(v_saved), flat(grad_out),
                           factors, crop_start, w_out, breadth)
    grid = kv.reshape(2, members, height, breadth, features)
    edges = jnp.stack([grid[:, :, :, :RADIUS], grid[:, :, :, -RADIUS:]])
    edges = edges.reshape(2, 2, members, height * RADIUS, features)
    rim_rows, sides = key_halos(kv, edges, breadth, rows, cols)
    o_t, dq, own, d_rows, d_sides = attend(q, do, kv, rim_rows, sides, breadth)
    rim_in, side_in, corner_in = returned_rims(d_rows, d_sides, rows, cols)
    gap = jnp.zeros((2, 2, members, (height - 2 * RADIUS) * RADIUS, features), BF16)
    side_in = side_in.astype(F32) + jnp.concatenate(
        [corner_in[:, 0], gap, corner_in[:, 1]], axis=3).astype(F32)
    side_in = side_in.reshape(2, 2, members, height, RADIUS, features)
    gap = jnp.zeros((2, members, height, breadth - 2 * RADIUS, features), F32)
    owned = own.reshape(grid.shape) + jnp.concatenate([side_in[0], gap, side_in[1]], axis=3)
    gap = jnp.zeros((2, members, cells - 2 * RADIUS * breadth, features), BF16)
    owned = owned.reshape(2, members, cells, features) + jnp.concatenate(
        [rim_in[0], gap, rim_in[1]], axis=2).astype(F32)
    owned = owned.astype(BF16).reshape(2, members * cells, features)
    grad_tokens, pieces = weight_pieces(
        tokens.reshape(-1, features), o_t, dq.reshape(-1, features), owned[0], owned[1],
        g.reshape(-1, features), w_qkv, rows, cols)
    part = reduce_pieces(pieces, rows, cols)
    split = 3 * features // cols
    return grad_tokens.reshape(tokens.shape), part[:, :split], part[:, split:]


def solution(mesh):
    placed = (
        P(None, "row", "col", None), P(), P(),
        P(None, "row", "col", None), P(None, "row", "col", None),
        P(None, "row", "col", None), P(None, "row", "col", None),
        P(None, "row", "col", None), P(),
    )
    return jax.shard_map(
        body, mesh=mesh, in_specs=placed,
        out_specs=(P(None, "row", "col", None), P("row", "col"), P("row", "col")),
        check_vma=False)
```

```python
import functools
import math

import jax
import jax.numpy as jnp
from jax import lax
from jax.experimental import pallas as pl
from jax.experimental.pallas import tpu as pltpu
from jax.sharding import PartitionSpec as P

HEADS = 8
RADIUS = 4
BLOCK = 8
PARTS = 2

max_norm = 1000.0
masked_score = -1e30
tiny_square = 1e-06
F32 = jnp.float32
BF16 = jnp.bfloat16


def dot(left, right, dims):
    return lax.dot_general(left, right, (dims, ((), ())), preferred_element_type=F32)


def prepare_kernel(q_ref, k_ref, v_ref, g_ref, fac_ref, crop_ref, w_ref,
                   q_out, kv_out, g_out, do_out, *, breadth):
    frame = pl.program_id(0)
    strip = pl.program_id(1)
    cells, features = q_ref.shape[1:]
    height = BLOCK * pl.num_programs(1)
    cell = lax.broadcasted_iota(jnp.int32, (cells, features), 0)
    block_col = (cell % breadth) // BLOCK

    def factor_of(which):
        factor = fac_ref[0, 0, 0:1, which * features:(which + 1) * features]
        full = jnp.broadcast_to(factor, (cells, features))
        for at in range(1, breadth // BLOCK):
            factor = fac_ref[0, 0, at:at + 1, which * features:(which + 1) * features]
            full = jnp.where(block_col == at, factor, full)
        return full

    q_out[0] = (q_ref[0].astype(F32) * factor_of(0)).astype(BF16)
    kv_out[0, 0] = (k_ref[0].astype(F32) * factor_of(1)).astype(BF16)
    kv_out[1, 0] = (v_ref[0].astype(F32) * factor_of(2)).astype(BF16)
    row = lax.axis_index("row") * height + strip * BLOCK + cell // breadth
    col = lax.axis_index("col") * breadth + cell % breadth
    inside = (row >= crop_ref[frame, 0]) & (col >= crop_ref[frame, 1])
    masked = jnp.where(inside, g_ref[0].astype(F32), 0.0).astype(BF16)
    g_out[0] = masked
    do_out[0] = dot(masked, w_ref[...], ((1,), (1,))).astype(BF16)


def prepare(q, k, v, g, factors, crop_start, w_out, breadth):
    members, cells, features = q.shape
    strip_cells = BLOCK * breadth
    strips = cells // strip_cells
    spec = pl.BlockSpec((1, strip_cells, features), lambda b, t: (b, t, 0))
    kv_spec = pl.BlockSpec((2, 1, strip_cells, features), lambda b, t: (0, b, t, 0))
    shape = jax.ShapeDtypeStruct(q.shape, BF16)
    return pl.pallas_call(
        functools.partial(prepare_kernel, breadth=breadth),
        grid=(members, strips),
        in_specs=[spec, spec, spec, spec,
                  pl.BlockSpec((1, 1) + factors.shape[2:], lambda b, t: (b, t, 0, 0)),
                  pl.BlockSpec(memory_space=pltpu.SMEM),
                  pl.BlockSpec(w_out.shape, lambda b, t: (0, 0))],
        out_specs=[spec, kv_spec, spec, spec],
        out_shape=[shape, jax.ShapeDtypeStruct((2,) + q.shape, BF16), shape, shape],
        name="prepare",
    )(q, k, v, g, factors, crop_start, w_out)


def attend_kernel(q_ref, do_ref, kv_ref, rows_ref, sides_ref, ot_ref, dq_ref, own_ref,
                  drows_ref, dsides_ref, bias_ref, *, breadth, head_dim):
    strip_cells = BLOCK * breadth
    rim_c = RADIUS * breadth
    side_cells = BLOCK * RADIUS
    cells = q_ref.shape[1]
    strips = cells // strip_cells
    keys_c, keys_s = 2 * strip_cells, 2 * side_cells
    keys = keys_c + 2 * keys_s
    lanes = q_ref.shape[2]
    stacked = (lanes // head_dim) * strip_cells
    height = strips * BLOCK

    @pl.when((pl.program_id(0) == 0) & (pl.program_id(1) == 0))
    def _():
        key = lax.broadcasted_iota(jnp.int32, (keys, stacked), 0)
        query = lax.broadcasted_iota(jnp.int32, (keys, stacked), 1) % strip_cells
        side = key - keys_c
        key_row = jnp.where(key < keys_c, key // breadth, (side % keys_s) // RADIUS) - RADIUS
        key_col = jnp.where(
            key < keys_c, key % breadth,
            side % RADIUS + jnp.where(side < keys_s, -RADIUS, breadth))
        d_row = key_row - query // breadth
        d_col = key_col - query % breadth
        near = (jnp.abs(d_row) <= RADIUS) & (jnp.abs(d_col) <= RADIUS)
        frame_rows = height * lax.axis_size("row")
        frame_cols = breadth * lax.axis_size("col")
        at_col = key_col + lax.axis_index("col") * breadth
        near = near & (at_col >= 0) & (at_col < frame_cols)
        for strip in range(strips):
            at_row = key_row + strip * BLOCK + lax.axis_index("row") * height
            seen = near & (at_row >= 0) & (at_row < frame_rows)
            bias_ref[strip] = jnp.where(seen, 0.0, masked_score)

    lane = lax.broadcasted_iota(jnp.int32, (strip_cells, lanes), 1)
    masks = [jnp.where(lane // head_dim == h, 1.0, 0.0).astype(BF16)
             for h in range(lanes // head_dim)]
    scale = 1.0 / math.sqrt(head_dim)

    def by_head(whole):
        return jnp.concatenate(
            [whole[h * head_dim:(h + 1) * head_dim, h * strip_cells:(h + 1) * strip_cells]
             for h in range(lanes // head_dim)], 0)

    def keys_of(which, strip):
        low, high = strip * strip_cells - rim_c, (strip + 2) * strip_cells - rim_c
        parts = [kv_ref[which, 0, max(low, 0):min(high, cells)]]
        if low < 0:
            parts.insert(0, rows_ref[0, which, 0])
        if high > cells:
            parts.append(rows_ref[1, which, 0])
        for side in range(2):
            parts.append(sides_ref[side, which, 0, strip * side_cells:strip * side_cells + keys_s])
        return jnp.concatenate(parts, 0)

    def put(which, chunk, center, sides):
        low = chunk * strip_cells - rim_c
        if chunk == 0:
            drows_ref[0, which, 0] = center[:rim_c].astype(BF16)
            own_ref[which, 0, :strip_cells - rim_c] = center[rim_c:]
        elif chunk == strips:
            own_ref[which, 0, low:] = center[:cells - low]
            drows_ref[1, which, 0] = center[cells - low:].astype(BF16)
        else:
            own_ref[which, 0, low:low + strip_cells] = center
        for side in range(2):
            dsides_ref[side, which, 0, chunk * side_cells:(chunk + 1) * side_cells] = (
                sides[side].astype(BF16))

    carry = None
    for strip in range(strips):
        at = slice(strip * strip_cells, (strip + 1) * strip_cells)
        q = q_ref[0, at] * scale
        g = do_ref[0, at]
        q_stack = jnp.concatenate([q * m for m in masks], 0)
        g_stack = jnp.concatenate([g * m for m in masks], 0)
        k, v = keys_of(0, strip), keys_of(1, strip)
        scores = dot(k, q_stack, ((1,), (1,))) + bias_ref[strip]
        weights = jnp.exp(scores - jnp.max(scores, axis=0, keepdims=True))
        softmax = weights * (1.0 / jnp.sum(weights, axis=0, keepdims=True))
        half = softmax.astype(BF16)
        grad_probs = dot(v, g_stack, ((1,), (1,)))
        delta = jnp.sum(softmax * grad_probs, axis=0, keepdims=True)
        grad_scores = (softmax * (grad_probs - delta)).astype(BF16)
        ot_ref[:, at] = by_head(dot(v, half, ((0,), (0,)))).astype(BF16)
        dq = by_head(dot(k, grad_scores, ((0,), (0,)))) * scale
        dq_ref[0, at] = dq.T.astype(BF16)
        parts = (dot(grad_scores, q_stack, ((1,), (0,))), dot(half, g_stack, ((1,), (0,))))
        after = []
        for which in range(2):
            pieces = [parts[which][:strip_cells]]
            rest = [parts[which][strip_cells:keys_c]]
            for side in range(2):
                first = keys_c + side * keys_s
                pieces.append(parts[which][first:first + side_cells])
                rest.append(parts[which][first + side_cells:first + keys_s])
            if carry is not None:
                pieces = [p + c for p, c in zip(pieces, carry[which])]
            put(which, strip, pieces[0], pieces[1:])
            after.append(rest)
        carry = after
    for which in range(2):
        put(which, strips, carry[which][0], carry[which][1:])


def attend(q, do, kv, rim_rows, sides, breadth):
    members, cells, features = q.shape
    head_dim = features // HEADS
    lanes = 128
    strips = cells // (BLOCK * breadth)
    keys = 2 * BLOCK * (breadth + 2 * RADIUS)
    stacked = (lanes // head_dim) * BLOCK * breadth
    spec = pl.BlockSpec((1, cells, lanes), lambda b, h: (b, 0, h))

    def kv_spec(array):
        lead = array.shape[:-3]
        return pl.BlockSpec(lead + (1, array.shape[-2], lanes),
                            lambda b, h: (0,) * len(lead) + (b, 0, h))

    return pl.pallas_call(
        functools.partial(attend_kernel, breadth=breadth, head_dim=head_dim),
        grid=(members, features // lanes),
        in_specs=[spec, spec, kv_spec(kv), kv_spec(rim_rows), kv_spec(sides)],
        out_specs=[pl.BlockSpec((lanes, cells), lambda b, h: (h, b)), spec,
                   kv_spec(kv), kv_spec(rim_rows), kv_spec(sides)],
        out_shape=[jax.ShapeDtypeStruct((features, members * cells), BF16),
                   jax.ShapeDtypeStruct(q.shape, BF16),
                   jax.ShapeDtypeStruct(kv.shape, F32),
                   jax.ShapeDtypeStruct(rim_rows.shape, BF16),
                   jax.ShapeDtypeStruct(sides.shape, BF16)],
        scratch_shapes=[pltpu.VMEM((strips, keys, stacked), F32)],
        name="attend",
    )(q, do, kv, rim_rows, sides)


DIRECTIONS = [(0, 1), (0, -1), (1, 0), (-1, 0), (1, 1), (1, -1), (-1, 1), (-1, -1)]


def exchange_kernel(*refs, rows, cols, inputs, table):
    arrays, (send_sem, recv_sem) = refs[:-2], refs[-2:]
    sources, targets = arrays[:inputs], arrays[inputs:]
    row, col = lax.axis_index("row"), lax.axis_index("col")

    def present(dr, dc):
        return ((row + dr >= 0) & (row + dr < rows) & (col + dc >= 0) & (col + dc < cols))

    barrier = pltpu.get_barrier_semaphore()
    met = 0
    for dr, dc in DIRECTIONS:
        there = present(dr, dc)

        @pl.when(there)
        def _(dr=dr, dc=dc):
            pl.semaphore_signal(barrier, inc=1, device_id=(row + dr, col + dc),
                                device_id_type=pl.DeviceIdType.MESH)

        met = met + there.astype(jnp.int32)
    pl.semaphore_wait(barrier, met)

    def copy_of(at):
        dr, dc = DIRECTIONS[at]
        source, source_at, target, target_at = table[dr, dc]
        return pltpu.make_async_remote_copy(
            src_ref=sources[source].at[source_at], dst_ref=targets[target].at[target_at],
            send_sem=send_sem.at[at], recv_sem=recv_sem.at[at],
            device_id=(row + dr, col + dc), device_id_type=pl.DeviceIdType.MESH)

    for at, (dr, dc) in enumerate(DIRECTIONS):
        @pl.when(present(dr, dc))
        def _(at=at):
            copy_of(at).start()

    for at, (dr, dc) in enumerate(DIRECTIONS):
        @pl.when(jnp.logical_not(present(-dr, -dc)))
        def _(at=at):
            _, _, target, target_at = table[DIRECTIONS[at]]
            view = targets[target].at[target_at]
            view[...] = jnp.zeros(view.shape, BF16)

    for at, (dr, dc) in enumerate(DIRECTIONS):
        @pl.when(present(dr, dc))
        def _(at=at):
            copy_of(at).wait_send()

        @pl.when(present(-dr, -dc))
        def _(at=at):
            copy_of(at).wait_recv()


def exchange(arrays, shapes, table, rows, cols, collective_id, name):
    return pl.pallas_call(
        functools.partial(exchange_kernel, rows=rows, cols=cols, inputs=len(arrays),
                          table=table),
        in_specs=[pl.BlockSpec(memory_space=pl.ANY)] * len(arrays),
        out_specs=[pl.BlockSpec(memory_space=pltpu.VMEM)] * len(shapes),
        out_shape=[jax.ShapeDtypeStruct(shape, BF16) for shape in shapes],
        scratch_shapes=[pltpu.SemaphoreType.DMA((8,)), pltpu.SemaphoreType.DMA((8,))],
        compiler_params=pltpu.CompilerParams(
            collective_id=collective_id, has_side_effects=True),
        name=name,
    )(*arrays)


def span(*lead, first=0, size):
    return lead + (slice(None), slice(None), pl.ds(first, size))


def key_halos(kv, edges, breadth, rows, cols):
    _, members, cells, features = kv.shape
    rim, corner, along = RADIUS * breadth, RADIUS * RADIUS, edges.shape[3]
    last = along - corner
    table = {
        (1, 0): (0, span(first=cells - rim, size=rim), 0, span(0, size=rim)),
        (-1, 0): (0, span(size=rim), 0, span(1, size=rim)),
        (0, 1): (1, span(1, size=along), 1, span(0, first=corner, size=along)),
        (0, -1): (1, span(0, size=along), 1, span(1, first=corner, size=along)),
        (1, 1): (1, span(1, first=last, size=corner), 1, span(0, size=corner)),
        (1, -1): (1, span(0, first=last, size=corner), 1, span(1, size=corner)),
        (-1, 1): (1, span(1, size=corner), 1, span(0, first=corner + along, size=corner)),
        (-1, -1): (1, span(0, size=corner), 1, span(1, first=corner + along, size=corner)),
    }
    shapes = [(2, 2, members, rim, features), (2, 2, members, along + 2 * corner, features)]
    return exchange([kv, edges], shapes, table, rows, cols, 2, "key_halos")


def returned_rims(d_rows, d_sides, rows, cols):
    _, _, members, rim, features = d_rows.shape
    corner = RADIUS * RADIUS
    along = d_sides.shape[3] - 2 * corner
    end = corner + along
    table = {
        (1, 0): (0, span(1, size=rim), 0, span(0, size=rim)),
        (-1, 0): (0, span(0, size=rim), 0, span(1, size=rim)),
        (0, 1): (1, span(1, first=corner, size=along), 1, span(0, size=along)),
        (0, -1): (1, span(0, first=corner, size=along), 1, span(1, size=along)),
        (1, 1): (1, span(1, first=end, size=corner), 2, span(0, 0, size=corner)),
        (1, -1): (1, span(0, first=end, size=corner), 2, span(1, 0, size=corner)),
        (-1, 1): (1, span(1, size=corner), 2, span(0, 1, size=corner)),
        (-1, -1): (1, span(0, size=corner), 2, span(1, 1, size=corner)),
    }
    shapes = [d_rows.shape, (2, 2, members, along, features),
              (2, 2, 2, members, corner, features)]
    return exchange([d_rows, d_sides], shapes, table, rows, cols, 3, "returned_rims")


def bits_of(count):
    return max(count.bit_length() - 1, 0)


def halving_orders(rows, cols):
    col = [("col", k) for k in range(bits_of(cols))]
    row = [("row", k) for k in range(bits_of(rows))]
    return [col[:1] + col[1:] + row, col[:1] + col[:0:-1] + row]


def place_of(order, row, col):
    place = 0
    for axis, bit in order:
        place = 2 * place + ((row if axis == "row" else col) // 2 ** bit) % 2
    return place


def weights_kernel(tok_ref, ot_ref, dq_ref, dk_ref, dv_ref, g_ref, w_ref,
                   dq_rows, dk_rows, dv_rows, gt_ref, buf_ref, *, orders, cols):
    features = g_ref.shape[1]
    tok = tok_ref[...]
    raw = jnp.concatenate(
        [dot(tok, ref[...], ((0,), (0,))) for ref in (dq_ref, dk_ref, dv_ref)], 1)
    raw_out = dot(ot_ref[...], g_ref[...], ((1,), (0,)))
    wide, narrow = 3 * features // cols, features // cols
    part_rows = buf_ref.shape[2]
    group = tok.shape[1] // (PARTS * part_rows)
    for member, col in ((m, c) for m in range(group) for c in range(cols)):
        row = pl.program_id(0) * group + member
        piece = jnp.concatenate(
            [raw[:, col * wide:(col + 1) * wide], raw_out[:, col * narrow:(col + 1) * narrow]],
            1).astype(BF16)
        for half, order in enumerate(orders):
            first = (PARTS * member + half) * part_rows
            buf_ref[half, place_of(order, row, col)] = piece[first:first + part_rows]
    total = dot(dq_rows[...], w_ref[:, :features], ((1,), (1,)))
    total = total + dot(dk_rows[...], w_ref[:, features:2 * features], ((1,), (1,)))
    total = total + dot(dv_rows[...], w_ref[:, 2 * features:], ((1,), (1,)))
    gt_ref[...] = total.astype(BF16)


def weight_pieces(tokens, o_t, dq, dk, dv, g, w_qkv, rows, cols):
    cells, features = tokens.shape
    orders = halving_orders(rows, cols)
    part_rows = features // rows
    group = max(1, 128 // part_rows)
    whole = pl.BlockSpec((cells, features), lambda r: (0, 0))
    some = pl.BlockSpec((cells * group // rows, features), lambda r: (r, 0))
    lanes = 4 * features // cols
    return pl.pallas_call(
        functools.partial(weights_kernel, orders=orders, cols=cols),
        grid=(rows // group,),
        in_specs=[pl.BlockSpec((cells, group * part_rows), lambda r: (0, r)),
                  pl.BlockSpec((group * part_rows, cells), lambda r: (r, 0)),
                  whole, whole, whole, whole,
                  pl.BlockSpec(w_qkv.shape, lambda r: (0, 0)), some, some, some],
        out_specs=[some, pl.BlockSpec((PARTS, rows * cols, part_rows // PARTS, lanes),
                                      lambda r: (0, 0, 0, 0))],
        out_shape=[jax.ShapeDtypeStruct((cells, features), BF16),
                   jax.ShapeDtypeStruct((PARTS, rows * cols, part_rows // PARTS, lanes), BF16)],
        name="weights",
    )(tokens, o_t, dq, dk, dv, g, w_qkv, dq, dk, dv)


def reduce_kernel(buf_ref, part_ref, work, recv, own_sq, all_sq,
                  send_sem, recv_sem, sq_send, sq_recv, *, rows, cols):
    orders = halving_orders(rows, cols)
    count = rows * cols
    mine = {"row": lax.axis_index("row"), "col": lax.axis_index("col")}
    me = mine["row"] * cols + mine["col"]

    def other(i):
        at = lax.rem(me + i, count)
        return (at // cols, at % cols)

    barrier = pltpu.get_barrier_semaphore()

    def greet(i, _):
        pl.semaphore_signal(barrier, inc=1, device_id=other(i),
                            device_id_type=pl.DeviceIdType.MESH)
        return 0

    lax.fori_loop(1, count, greet, 0)
    pl.semaphore_wait(barrier, count - 1)
    steps = len(orders[0])
    base = [0] * PARTS
    finals = [None] * PARTS

    def start(half, step):
        axis, bit = orders[half][step]
        size = count >> (step + 1)
        mybit = (mine[axis] // 2 ** bit) % 2
        partner = dict(mine)
        partner[axis] = mine[axis] + (1 - 2 * mybit) * 2 ** bit
        source = buf_ref if step == 0 else work
        at = recv.at[half, pl.ds(count - 2 * size, size)]
        copy = pltpu.make_async_remote_copy(
            src_ref=source.at[half, pl.ds(base[half] + (1 - mybit) * size, size)],
            dst_ref=at, send_sem=send_sem.at[half, step], recv_sem=recv_sem.at[half, step],
            device_id=(partner["row"], partner["col"]),
            device_id_type=pl.DeviceIdType.MESH)
        copy.start()
        return copy, size, mybit

    flights = [start(half, 0) for half in range(PARTS)]
    for step in range(steps):
        for half in range(PARTS):
            copy, size, mybit = flights[half]
            copy.wait()
            keep = base[half] + mybit * size
            first = count - 2 * size
            if step == steps - 1:
                finals[half] = work[half, keep].astype(F32) + recv[half, first].astype(F32)
                continue
            source = buf_ref if step == 0 else work
            base[half] = 0 if step == 0 else keep

            work[half, pl.ds(base[half], size)] = (
                source[half, pl.ds(keep, size)] + recv[half, pl.ds(first, size)])
            flights[half] = start(half, step + 1)
    part = jnp.concatenate(finals, 0)
    squares = jnp.sum((part * part).reshape(-1, 8, part.shape[1]), axis=0)
    tile = own_sq.shape[1]
    own_sq[...] = sum(squares[:, j * tile:(j + 1) * tile] for j in range(part.shape[1] // tile))

    def square_copy(i):
        return pltpu.make_async_remote_copy(
            src_ref=own_sq, dst_ref=all_sq.at[i], send_sem=sq_send.at[i],
            recv_sem=sq_recv.at[i], device_id=other(i),
            device_id_type=pl.DeviceIdType.MESH)

    def send(i, _):
        square_copy(i).start()
        return 0

    def take(i, total):
        square_copy(i).wait()
        return total + all_sq[i]

    lax.fori_loop(1, count, send, 0)
    total = jnp.sum(lax.fori_loop(1, count, take, own_sq[...]), keepdims=True)
    factor = jnp.minimum(1.0, max_norm / jnp.sqrt(total + tiny_square))
    part_ref[...] = (part * factor).T


def reduce_pieces(pieces, rows, cols):
    count = rows * cols
    half_rows, lanes = pieces.shape[2:]
    steps = bits_of(count)
    vmem = pl.BlockSpec(memory_space=pltpu.VMEM)
    return pl.pallas_call(
        functools.partial(reduce_kernel, rows=rows, cols=cols),
        in_specs=[vmem], out_specs=vmem,
        out_shape=jax.ShapeDtypeStruct((lanes, PARTS * half_rows), F32),
        scratch_shapes=[
            pltpu.VMEM((PARTS, count // 2, half_rows, lanes), BF16),
            pltpu.VMEM((PARTS, count, half_rows, lanes), BF16),
            pltpu.VMEM((8, 128), F32), pltpu.VMEM((count, 8, 128), F32),
            pltpu.SemaphoreType.DMA((PARTS, steps)),
            pltpu.SemaphoreType.DMA((PARTS, steps)),
            pltpu.SemaphoreType.DMA((count,)), pltpu.SemaphoreType.DMA((count,))],
        compiler_params=pltpu.CompilerParams(collective_id=1, has_side_effects=True),
        name="reduce",
    )(pieces)


def passed_along(array, axis, by):
    size = lax.axis_size(axis)
    return lax.ppermute(
        array, axis, [(i, i + by) for i in range(size) if 0 <= i + by < size])


def body(tokens, w_qkv, w_out, q_saved, k_saved, v_saved, scale_exp, grad_out, crop_start):
    members, height, breadth, features = tokens.shape
    cells = height * breadth
    rows, cols = lax.axis_size("row"), lax.axis_size("col")
    factors = jnp.repeat(jnp.exp2(scale_exp.astype(F32)), features // HEADS, axis=3)

    def flat(array):
        return array.reshape(members, cells, features)

    q, kv, g, do = prepare(flat(q_saved), flat(k_saved), flat(v_saved), flat(grad_out),
                           factors, crop_start, w_out, breadth)
    grid = kv.reshape(2, members, height, breadth, features)
    edges = jnp.stack([grid[:, :, :, :RADIUS], grid[:, :, :, -RADIUS:]])
    edges = edges.reshape(2, 2, members, height * RADIUS, features)
    rim_rows, sides = key_halos(kv, edges, breadth, rows, cols)
    o_t, dq, own, d_rows, d_sides = attend(q, do, kv, rim_rows, sides, breadth)
    rim_in, side_in, corner_in = returned_rims(d_rows, d_sides, rows, cols)
    gap = jnp.zeros((2, 2, members, (height - 2 * RADIUS) * RADIUS, features), BF16)
    side_in = side_in.astype(F32) + jnp.concatenate(
        [corner_in[:, 0], gap, corner_in[:, 1]], axis=3).astype(F32)
    side_in = side_in.reshape(2, 2, members, height, RADIUS, features)
    gap = jnp.zeros((2, members, height, breadth - 2 * RADIUS, features), F32)
    owned = own.reshape(grid.shape) + jnp.concatenate([side_in[0], gap, side_in[1]], axis=3)
    gap = jnp.zeros((2, members, cells - 2 * RADIUS * breadth, features), BF16)
    owned = owned.reshape(2, members, cells, features) + jnp.concatenate(
        [rim_in[0], gap, rim_in[1]], axis=2).astype(F32)
    owned = owned.astype(BF16).reshape(2, members * cells, features)
    grad_tokens, pieces = weight_pieces(
        tokens.reshape(-1, features), o_t, dq.reshape(-1, features), owned[0], owned[1],
        g.reshape(-1, features), w_qkv, rows, cols)
    part = reduce_pieces(pieces, rows, cols)
    split = 3 * features // cols
    return grad_tokens.reshape(tokens.shape), part[:split].T, part[split:].T


def solution(mesh):
    placed = (
        P(None, "row", "col", None), P(), P(),
        P(None, "row", "col", None), P(None, "row", "col", None),
        P(None, "row", "col", None), P(None, "row", "col", None),
        P(None, "row", "col", None), P(),
    )
    return jax.shard_map(
        body, mesh=mesh, in_specs=placed,
        out_specs=(P(None, "row", "col", None), P("row", "col"), P("row", "col")),
        check_vma=False)
```
